128 devices in a mesh: gx: 4 (over y), gy: 4 (over x_lo, core), gz: 8 (over x_hi, z).
Axes of the slice: x: 4 (x_hi: 2, x_lo: 2; x = x_hi * 2 + x_lo), y: 4, z: 4, core: 2. Of those that a mesh axis runs over, the one named last changes fastest.
Arguments:
- inputs: bfloat16 [112, 112, 56, 96], P('gx', 'gy', 'gz'), may hold values from -6 to 6
- d_out: bfloat16 [112, 112, 56, 96], P('gx', 'gy', 'gz'), may hold values from -6 to 6
- layer_norm_gain: float32 [96], replicated, may hold values from 0.1 to 1.9
- layer_norm_bias: float32 [96], replicated, may hold values from -3 to 3
- w_qkv: bfloat16 [96, 288], replicated, may hold values from -0.625 to 0.625
- b_qkv: float32 [288], replicated, may hold values from -3 to 3
- w_proj: bfloat16 [96, 96], replicated, may hold values from -0.625 to 0.625
- rel_bias: float32 [3, 2197], replicated, may hold values from -4 to 240
Outputs:
- d_x: bfloat16 [112, 112, 56, 96], P('gx', 'gy', 'gz')
- g_qkv: float32 [96, 288], replicated
- g_bqkv: float32 [288], replicated
- g_proj: float32 [96, 96], replicated
- g_rel: float32 [3, 2197], replicated
- gain_gradient: float32 [96], replicated
- g_shift: float32 [96], replicated
The draws below stay inside these ranges and needn't reach their ends.
All inputs are finite; a program needn't handle non-finite values.
Results may differ from the reference program's by a relative error of at most 0.011.
Values may be sent and summed in bfloat16 or wider, within the bound.
A program may use at most 192 MiB of HBM per device.

```python
import jax
import jax.numpy as jnp
import numpy as np
from jax import lax

C = 96
HEADS = 3
WIN = 7
SHIFT = 3
NX = 112
NY = 112
NZ = 56
TOKENS = 702464
TABLE = 2197


def draw_rel_bias(key, part):
    first = jax.random.fold_in(jax.random.fold_in(key, 17), 0)
    width = 2 * WIN - 1
    return jnp.clip(jax.random.normal(first, (HEADS, width ** 3), jnp.float32), -4.0, 4.0)


def shard_levels(rng, extent, shards, low, high):
    def one(axis_at, shards_of):
        steps = jax.random.uniform(jax.random.fold_in(jax.random.fold_in(rng, 6), axis_at), (shards_of,), jnp.float32, low / len(shards), high / len(shards))
        return jnp.repeat(jnp.exp(steps), extent[axis_at] // shards_of).reshape((-1,) + (1,) * (len(extent) - axis_at - 1))

    loudness = one(*shards[0])
    for cut in shards[1:]:
        loudness = loudness * one(*cut)
    return loudness


def scatter_about(stream_key, extent, spread, reach, pieces=(), dtype=jnp.bfloat16):
    result = spread * jax.random.normal(stream_key, extent, jnp.float32)
    if pieces:
        result = result * shard_levels(stream_key, extent, pieces, -0.22, 0.18)
    return jnp.clip(result, -reach, reach).astype(dtype)


def setup_inputs(seed: int = 0) -> dict:
    key_list = jax.random.split(jax.random.key(seed), 9)
    return {
        "inputs": scatter_about(key_list[0], (NX, NY, NZ, C), 1.0, 6.0, ((0, 4), (1, 4), (2, 8))),
        "d_out": scatter_about(key_list[1], (NX, NY, NZ, C), 1.0, 6.0, ((0, 4), (1, 4), (2, 8))),
        "layer_norm_gain": jnp.clip(1.0 + 0.18 * jax.random.normal(key_list[2], (C,), jnp.float32), 0.1, 1.9),
        "layer_norm_bias": scatter_about(key_list[3], (C,), 0.5, 3.0, (), jnp.float32),
        "w_qkv": scatter_about(key_list[4], (C, 3 * C), C ** -0.5, 0.625),
        "b_qkv": scatter_about(key_list[5], (3 * C,), 0.5, 3.0, (), jnp.float32),
        "w_proj": scatter_about(key_list[6], (C, C), C ** -0.5, 0.625),
        "rel_bias": draw_rel_bias(jax.random.fold_in(key_list[8], 71), 0),
    }


def relative_index(span):
    coords = np.stack(np.meshgrid(np.arange(span), np.arange(span), np.arange(span), indexing='ij'), -1).reshape(-1, 3)
    offset = coords[:, None, :] - coords[None, :, :] + span - 1
    width = 2 * span - 1
    return (offset[..., 0] * width * width + offset[..., 1] * width + offset[..., 2]).reshape(-1).astype(np.int32)

def region_label(count):
    places = jnp.arange(count)
    return jnp.where(places < count - WIN, 0, jnp.where(places < count - SHIFT, 1, 2)).astype(jnp.int32)

def to_windows(array):
    first, second, third = array.shape[:3]
    rest = array.shape[3:]
    shaped = array.reshape((first // WIN, WIN, second // WIN, WIN, third // WIN, WIN) + rest)
    order = (0, 2, 4, 1, 3, 5) + tuple(range(6, 6 + len(rest)))
    return shaped.transpose(order).reshape((-1, WIN ** 3) + rest)

def from_windows(array, first, second, third):
    feats = array.shape[-1]
    shaped = array.reshape(first // WIN, second // WIN, third // WIN, WIN, WIN, WIN, feats)
    return shaped.transpose(0, 3, 1, 4, 2, 5, 6).reshape(first, second, third, feats)

def window_pass(ln_w, dy_w, lab_w, w_qkv, b_qkv, w_proj, bias_full):
    f32 = jnp.float32
    bf16 = jnp.bfloat16
    group, tok, feats = ln_w.shape
    heads = bias_full.shape[0]
    hdim = feats // heads
    scale = hdim ** (-0.5)
    qkv = jnp.einsum('gtc,cf->gtf', ln_w.astype(f32), w_qkv.astype(f32)) + b_qkv
    qkv = qkv.astype(bf16).reshape(group, tok, 3, heads, hdim)
    query = qkv[:, :, 0].transpose(0, 2, 1, 3).astype(f32)
    keys = qkv[:, :, 1].transpose(0, 2, 1, 3).astype(f32)
    values = qkv[:, :, 2].transpose(0, 2, 1, 3).astype(f32)
    scores = jnp.einsum('ghid,ghjd->ghij', query, keys) * scale + bias_full[None]
    allowed = (lab_w[:, :, None] == lab_w[:, None, :])[:, None]
    scores = jnp.where(allowed, scores, f32(-1e+30))
    top = lax.optimization_barrier(jnp.max(scores, -1, keepdims=True))
    expo = jnp.exp(scores - top)
    probs = expo / lax.optimization_barrier(jnp.sum(expo, -1, keepdims=True))
    probs_b = probs.astype(bf16).astype(f32)
    attended = jnp.einsum('ghij,ghjd->ghid', probs_b, values)
    attended = attended.transpose(0, 2, 1, 3).reshape(group, tok, feats).astype(bf16).astype(f32)
    grad_att = jnp.einsum('gtc,fc->gtf', dy_w.astype(f32), w_proj.astype(f32)).astype(bf16).astype(f32)
    proj_part = jnp.einsum('gtf,gtc->fc', attended, dy_w.astype(f32))
    grad_heads = grad_att.reshape(group, tok, heads, hdim).transpose(0, 2, 1, 3)
    grad_probs = jnp.einsum('ghid,ghjd->ghij', grad_heads, values)
    grad_v = jnp.einsum('ghij,ghid->ghjd', probs_b, grad_heads)
    grad_scores = probs * (grad_probs - lax.optimization_barrier(jnp.sum(probs * grad_probs, -1, keepdims=True)))
    rel_part = lax.optimization_barrier(jnp.sum(grad_scores, 0))
    scores_b = grad_scores.astype(bf16).astype(f32)
    grad_q = jnp.einsum('ghij,ghjd->ghid', scores_b, keys) * scale
    grad_k = jnp.einsum('ghij,ghid->ghjd', scores_b, query) * scale
    grad_qkv = jnp.stack([grad_q, grad_k, grad_v], 1).transpose(0, 3, 1, 2, 4).reshape(group, tok, 3 * feats)
    bias_part = lax.optimization_barrier(jnp.sum(grad_qkv, (0, 1)))
    qkv_b = grad_qkv.astype(bf16).astype(f32)
    weight_part = jnp.einsum('gtc,gtf->cf', ln_w.astype(f32), qkv_b)
    grad_in = jnp.einsum('gtf,cf->gtc', qkv_b, w_qkv.astype(f32))
    return (grad_in, (weight_part, bias_part, proj_part, rel_part))

def reference(inputs, d_out, layer_norm_gain, layer_norm_bias, w_qkv, b_qkv, w_proj, rel_bias):
    f32 = jnp.float32
    tok = WIN ** 3
    feats = inputs.shape[-1]
    xf = inputs.astype(f32)
    centered_input = xf - lax.optimization_barrier(jnp.mean(xf, -1, keepdims=True))
    inverse_deviation = lax.rsqrt(lax.optimization_barrier(jnp.mean(centered_input * centered_input, -1, keepdims=True)) + 1e-05)
    normalized_input = centered_input * inverse_deviation
    normalized_tokens = (normalized_input * layer_norm_gain + layer_norm_bias).astype(jnp.bfloat16)
    moved = jnp.roll(normalized_tokens, (-SHIFT, -SHIFT, -SHIFT), (0, 1, 2))
    grad_moved = jnp.roll(d_out, (-SHIFT, -SHIFT, -SHIFT), (0, 1, 2))
    labels = region_label(NX)[:, None, None] * 9 + region_label(NY)[None, :, None] * 3 + region_label(NZ)[None, None, :]
    index = jnp.asarray(relative_index(WIN)).astype(jnp.int32)
    bias_full = jnp.take(rel_bias, index, axis=1).reshape(HEADS, tok, tok)
    group = NZ // WIN
    win_ln = to_windows(moved).reshape(-1, group, tok, feats)
    win_dy = to_windows(grad_moved).reshape(-1, group, tok, feats)
    win_lab = to_windows(labels).reshape(-1, group, tok)

    def step(carry, item):
        grad_in, parts = window_pass(item[0], item[1], item[2], w_qkv, b_qkv, w_proj, bias_full)
        return (tuple((total + part for total, part in zip(carry, parts))), grad_in)
    start = (jnp.zeros((feats, 3 * feats), f32), jnp.zeros((3 * feats,), f32), jnp.zeros((feats, feats), f32), jnp.zeros((HEADS, tok, tok), f32))
    sums, grad_win = lax.scan(step, start, (win_ln, win_dy, win_lab))
    grad_in = from_windows(grad_win.reshape(-1, tok, feats), NX, NY, NZ)
    normalized_output_gradient = jnp.roll(grad_in, (SHIFT, SHIFT, SHIFT), (0, 1, 2))
    normalized_gradient = normalized_output_gradient * layer_norm_gain
    input_gradient_norm = inverse_deviation * (normalized_gradient - lax.optimization_barrier(jnp.mean(normalized_gradient, -1, keepdims=True)) - normalized_input * lax.optimization_barrier(jnp.mean(normalized_gradient * normalized_input, -1, keepdims=True)))
    d_x = (d_out.astype(f32) + input_gradient_norm).astype(jnp.bfloat16)
    rel_sum = jax.ops.segment_sum(sums[3].reshape(HEADS, -1).T, index, num_segments=TABLE).T
    inverse_width_factor = float(TOKENS) ** (-0.5)
    gain_gradient = lax.optimization_barrier(jnp.sum(normalized_output_gradient * normalized_input, (0, 1, 2))) * inverse_width_factor
    g_shift = lax.optimization_barrier(jnp.sum(normalized_output_gradient, (0, 1, 2))) * inverse_width_factor
    return (d_x, sums[0] * inverse_width_factor, sums[1] * inverse_width_factor, sums[2] * inverse_width_factor, rel_sum * inverse_width_factor, gain_gradient, g_shift)
```

```python
import functools

import jax
import jax.numpy as jnp
import numpy as np
from jax import lax
from jax.experimental import pallas as pl
from jax.experimental.pallas import tpu as pltpu
from jax.sharding import PartitionSpec as P

WIN = 7
SHIFT = 3
TOK = WIN**3
ROWS = 352
LANES = 384
FEATS = 96
HEADS = 3
HDIM = 32
PLANE = 49
WIDTH = 13
TABLE = WIDTH**3
SPREAD = 2304
SQUEEZED = 640
FAR = -(2.0**100)
NEVER = -1e30
LOG2E = 1.4426950408889634
SCALE = HDIM**-0.5
F32 = jnp.float32
BF16 = jnp.bfloat16


def nn(a, b):
    return lax.dot_general(a, b, (((1,), (0,)), ((), ())), preferred_element_type=F32)


def nt(a, b):
    return lax.dot_general(a, b, (((1,), (1,)), ((), ())), preferred_element_type=F32)


def squeeze_ones():
    lane = np.arange(SQUEEZED)
    place = lane // 49 * 169 + lane % 49 // 7 * 13 + lane % 7
    return (np.arange(SPREAD)[:, None] == np.where(lane < 637, place, -1)[None, :]).astype(np.float32)


def token_features():
    token = np.arange(ROWS)
    late = np.stack([token // 49 >= 4, token % 49 // 7 >= 4, token % 7 >= 4]).astype(np.float32)
    return late


def key_features():
    late = token_features()
    out = np.zeros((ROWS, 256), np.float32)
    for d in range(3):
        out[:, 96 + 2 * d] = late[d]
        out[:, 97 + 2 * d] = 1 - late[d]
    return out


def query_features():
    token = np.arange(LANES)
    late = np.stack([token // 49 >= 4, token % 49 // 7 >= 4, token % 7 >= 4]).astype(np.float32)
    out = np.zeros((3, 16, LANES), np.float32)
    for d in range(3):
        out[d, 2 * d] = FAR * (1 - late[d])
        out[d, 2 * d + 1] = FAR * late[d]
    return out


def pieces(x, count):
    out = []
    for _ in range(count):
        piece = x.astype(BF16)
        out.append(piece)
        x = x - piece.astype(F32)
    return out


def expand_table(table_ref, ones_ref, bias_ref, wide_ref, flat_ref):
    for h in range(HEADS):
        row = jnp.broadcast_to(table_ref[h : h + 1, :] * LOG2E, (8, SPREAD))
        row = pltpu.roll(row, 0, 1, stride=1, stride_axis=0)
        for jy in range(WIN):
            moved = pltpu.roll(row, SPREAD - 13 * (6 - jy) - 6, 1)
            for n, piece in enumerate(pieces(moved, 3)):
                wide_ref[n, h * 56 + jy * 8 : h * 56 + jy * 8 + 8, :] = piece.astype(F32)
    total = None
    for n in range(3):
        part = nn(wide_ref[n].astype(BF16), ones_ref[...])
        total = part if total is None else total + part
    flat_ref[...] = total
    lane = lax.broadcasted_iota(jnp.int32, (8, LANES), 1)
    for h in range(HEADS):
        for jx in range(WIN):
            turned = pltpu.roll(flat_ref[h * 56 : h * 56 + 56, :], (SQUEEZED - 49 * (6 - jx)) % SQUEEZED, 1)
            for jy in range(WIN):
                bias_ref[h, pl.ds(jx * 49 + jy * 7, 8), :] = jnp.where(
                    lane < TOK, turned[jy * 8 : jy * 8 + 8, :LANES], 0.0
                )
        bias_ref[h, TOK : TOK + 9, :] = jnp.full((9, LANES), NEVER, F32)


def fold_table(sums_ref, ones_ref, wide_ref, flat_ref, out_ref):
    flat_ref[...] = jnp.zeros((HEADS * 56, SQUEEZED), F32)
    sub = lax.broadcasted_iota(jnp.int32, (8, SQUEEZED), 0)
    for h in range(HEADS):
        for jy in range(WIN):
            total = jnp.zeros((8, SQUEEZED), F32)
            for jx in range(WIN):
                block = sums_ref[h, pl.ds(jx * 49 + jy * 7, 8), :]
                block = jnp.concatenate([block, jnp.zeros((8, SQUEEZED - LANES), F32)], 1)
                total = total + pltpu.roll(block, 49 * (6 - jx), 1)
            flat_ref[h * 56 + jy * 8 : h * 56 + jy * 8 + 8, :] = jnp.where(sub < WIN, total, 0.0)
    spread = None
    for piece in pieces(flat_ref[...], 3):
        part = nt(piece, ones_ref[...])
        spread = part if spread is None else spread + part
    wide_ref[0] = spread
    for h in range(HEADS):
        total = jnp.zeros((8, SPREAD), F32)
        for jy in range(WIN):
            block = wide_ref[0, h * 56 + jy * 8 : h * 56 + jy * 8 + 8, :]
            total = total + pltpu.roll(block, 13 * (6 - jy), 1)
        line = jnp.zeros((1, SPREAD), F32)
        for jz in range(WIN):
            line = line + pltpu.roll(total, 6 - jz, 1)[jz : jz + 1]
        out_ref[h : h + 1, :] = line


def window_kernel(
    cells_x,
    cells_y,
    x_ref,
    dy_ref,
    gain_ref,
    shift_ref,
    table_ref,
    ones_ref,
    w_all_ref,
    w_kv_ref,
    b_col_ref,
    b_kv_ref,
    q_feat_ref,
    w_proj_ref,
    w_qkv_ref,
    dx_ref,
    wq_ref,
    wkv_ref,
    proj_ref,
    rel_ref,
    rows_ref,
    bq_ref,
    bias_ref,
    acc_ref,
    e_ref,
    ds_ref,
    q_ref,
    do_ref,
    ln_ref,
    gq_ref,
    wide_ref,
    flat_ref,
):
    step = pl.program_id(0)

    @pl.when(step == 0)
    def _():
        expand_table(table_ref, ones_ref, bias_ref, wide_ref, flat_ref)
        acc_ref[...] = jnp.zeros_like(acc_ref)
        e_ref[...] = jnp.zeros_like(e_ref)
        ds_ref[...] = jnp.zeros_like(ds_ref)
        q_ref[...] = jnp.zeros_like(q_ref)
        do_ref[...] = jnp.zeros_like(do_ref)
        wq_ref[...] = jnp.zeros_like(wq_ref)
        wkv_ref[...] = jnp.zeros_like(wkv_ref)
        proj_ref[...] = jnp.zeros_like(proj_ref)
        rows_ref[...] = jnp.zeros_like(rows_ref)
        bq_ref[...] = jnp.zeros_like(bq_ref)
        gq_ref[...] = jnp.zeros_like(gq_ref)
        ln_ref[...] = jnp.zeros_like(ln_ref)

    wins_y = cells_y // WIN
    wins_x = cells_x // WIN
    last_x = (lax.axis_index("gx") == lax.axis_size("gx") - 1) & (step // wins_y == wins_x - 1)
    last_y = (lax.axis_index("gy") == lax.axis_size("gy") - 1) & (step % wins_y == wins_y - 1)
    last_z = lax.axis_index("gz") == lax.axis_size("gz") - 1

    x = x_ref[0].astype(F32)
    mean = jnp.mean(x, -1, keepdims=True)
    centered = x - mean
    rstd = lax.rsqrt(jnp.mean(centered * centered, -1, keepdims=True) + 1e-05)
    xhat = centered * rstd
    ln_ref[0:ROWS, :] = (xhat * gain_ref[...] + shift_ref[...]).astype(BF16)

    across = nt(w_all_ref[...], ln_ref[...])
    q_t = ((across[0:96] + b_col_ref[0:96]) * (SCALE * LOG2E)).astype(BF16)
    k_t = (across[96:192] + b_col_ref[96:192]).astype(BF16)
    v_t = (across[192:288] + b_col_ref[192:288]).astype(BF16)
    ln_t = across[288:384].astype(BF16)
    marks = (
        q_feat_ref[0] * last_x.astype(F32)
        + q_feat_ref[1] * last_y.astype(F32)
        + q_feat_ref[2] * last_z.astype(F32)
    ).astype(BF16)
    for h in range(HEADS):
        q_ref[h * HDIM : (h + 1) * HDIM, h * LANES : (h + 1) * LANES] = q_t[h * HDIM : (h + 1) * HDIM]
        q_ref[96:112, h * LANES : (h + 1) * LANES] = marks
    kv = nn(ln_ref[0:ROWS, :], w_kv_ref[...]) + b_kv_ref[...]
    k = kv[:, 0:128].astype(BF16)
    v = kv[:, 128:256].astype(BF16)
    dy = dy_ref[0]
    do_t = nt(w_proj_ref[...], dy)

    att = []
    for h in range(HEADS):
        inverse = []
        for c in range(3):
            at = pl.ds(h * LANES + c * 128, 128)
            s = nn(k, q_ref[:, at]) + bias_ref[h, :, pl.ds(c * 128, 128)]
            e = jnp.exp2(s - jnp.max(s, 0, keepdims=True))
            inv = 1.0 / jnp.sum(e, 0, keepdims=True)
            inverse.append(inv)
            e_ref[0:ROWS, at] = e.astype(BF16)
            do_ref[h * HDIM : (h + 1) * HDIM, at] = (
                do_t[h * HDIM : (h + 1) * HDIM, c * 128 : c * 128 + 128] * inv
            ).astype(BF16)
            dp = nn(v, do_ref[:, at])
            ds = e * (dp - jnp.sum(e * dp, 0, keepdims=True) * inv)
            acc_ref[h, :, pl.ds(c * 128, 128)] += ds
            ds_ref[0:ROWS, at] = ds.astype(BF16)
        at = pl.ds(h * LANES, LANES)
        inverse = jnp.concatenate(inverse, 1)
        o_t = nn(v_t[h * HDIM : (h + 1) * HDIM], e_ref[:, at]) * inverse
        att.append(o_t.astype(BF16))
        gq_ref[h * HDIM : (h + 1) * HDIM, :] = nn(k_t[h * HDIM : (h + 1) * HDIM], ds_ref[:, at]) * SCALE
    att = jnp.concatenate(att, 0)
    proj_ref[...] += nn(att, dy)
    grad_v = nt(e_ref[0:ROWS, :], do_ref[...])
    grad_k = nt(ds_ref[0:ROWS, :], q_ref[0:96, :]) * (1.0 / LOG2E)
    gq = gq_ref[...]
    bq_ref[...] += gq[0:96, 0:128] + gq[0:96, 128:256] + gq[0:96, 256:384]
    wq_ref[...] += nn(gq[0:96].astype(BF16), ln_ref[...])
    grad_q = gq.T[0:ROWS, 0:96].astype(BF16)
    grad_v = grad_v[:, 0:96]
    k_b = grad_k.astype(BF16)
    v_b = grad_v.astype(BF16)
    wkv_ref[:, 0:96] += nn(ln_t[:, 0:ROWS], k_b)
    wkv_ref[:, 128:224] += nn(ln_t[:, 0:ROWS], v_b)
    grad_in = (
        nt(grad_q, w_qkv_ref[:, 0:96])
        + nt(k_b, w_qkv_ref[:, 128:224])
        + nt(v_b, w_qkv_ref[:, 256:352])
    )
    rows_ref[0] += jnp.sum(grad_k.reshape(ROWS // 8, 8, 96), 0)
    rows_ref[1] += jnp.sum(grad_v.reshape(ROWS // 8, 8, 96), 0)
    rows_ref[2] += jnp.sum((xhat * grad_in).reshape(ROWS // 8, 8, 96), 0)
    rows_ref[3] += jnp.sum(grad_in.reshape(ROWS // 8, 8, 96), 0)
    dhat = grad_in * gain_ref[...]
    first = jnp.mean(dhat, -1, keepdims=True)
    second = jnp.mean(dhat * xhat, -1, keepdims=True)
    dx_ref[0] = (dy[0:ROWS].astype(F32) + rstd * (dhat - first - xhat * second)).astype(BF16)

    @pl.when(step == pl.num_programs(0) - 1)
    def _():
        fold_table(acc_ref, ones_ref, wide_ref, flat_ref, rel_ref)


def window_call(win_x, win_dy, gain, shift, table, w_qkv, b_qkv, w_proj, cells_x, cells_y):
    count = win_x.shape[0]
    ones = jnp.asarray(squeeze_ones(), BF16)
    w_t = w_qkv.T
    w_all = jnp.concatenate([w_t, jnp.eye(96, dtype=BF16)], 0)
    gap = jnp.zeros((96, 32), BF16)
    w_k, w_v = w_qkv[:, 96:192], w_qkv[:, 192:288]
    w_kv = jnp.concatenate([w_k, gap, w_v, gap], 1)
    w_back = jnp.concatenate([w_qkv[:, 0:96], gap, w_k, gap, w_v, gap], 1)
    gap_b = jnp.zeros((32,), F32)
    b_row = jnp.concatenate([b_qkv[96:192], gap_b, b_qkv[192:288], gap_b])
    b_kv = jnp.asarray(key_features()) + b_row[None, :]
    b_col = b_qkv[:, None]
    table = jnp.pad(table, ((0, 5), (0, SPREAD - TABLE)))
    whole = lambda a: pl.BlockSpec(a.shape, lambda i: (0,) * a.ndim)
    tile = lambda rows: pl.BlockSpec((1, rows, FEATS), lambda i: (i, 0, 0))
    consts = (gain[None, :], shift[None, :], table, ones, w_all, w_kv, b_col, b_kv)
    consts += (jnp.asarray(query_features()), w_proj, w_back)
    outs = (
        jax.ShapeDtypeStruct((count, ROWS, FEATS), BF16),
        jax.ShapeDtypeStruct((96, 96), F32),
        jax.ShapeDtypeStruct((96, 256), F32),
        jax.ShapeDtypeStruct((96, 96), F32),
        jax.ShapeDtypeStruct((8, SPREAD), F32),
        jax.ShapeDtypeStruct((4, 8, 96), F32),
        jax.ShapeDtypeStruct((96, 128), F32),
    )
    return pl.pallas_call(
        functools.partial(window_kernel, cells_x, cells_y),
        grid=(count,),
        in_specs=[tile(LANES)] * 0 + [tile(ROWS), tile(LANES)] + [whole(a) for a in consts],
        out_specs=[tile(ROWS)] + [whole(a) for a in outs[1:]],
        out_shape=outs,
        scratch_shapes=[
            pltpu.VMEM((HEADS, ROWS, LANES), F32),
            pltpu.VMEM((HEADS, ROWS, LANES), F32),
            pltpu.VMEM((LANES, HEADS * LANES), BF16),
            pltpu.VMEM((LANES, HEADS * LANES), BF16),
            pltpu.VMEM((128, HEADS * LANES), BF16),
            pltpu.VMEM((128, HEADS * LANES), BF16),
            pltpu.VMEM((LANES, FEATS), BF16),
            pltpu.VMEM((128, LANES), F32),
            pltpu.VMEM((3, HEADS * 56, SPREAD), F32),
            pltpu.VMEM((HEADS * 56, SQUEEZED), F32),
        ],
        compiler_params=pltpu.CompilerParams(vmem_limit_bytes=56 << 20),
        cost_estimate=pl.CostEstimate(flops=5 * 10**9, bytes_accessed=6 * 10**6, transcendentals=6 * 10**6),
    )(win_x, win_dy, *consts)


def shifted(block, axis, distance):
    devices = range(lax.axis_size(axis))
    route = [((i - distance) % len(devices), i) for i in devices]
    return lax.ppermute(block, axis, route)


def in_one(arrays, axis):
    ends = [0]
    for a in arrays:
        ends.append(ends[-1] + a.size)
    so_far = lax.psum(jnp.concatenate([a.ravel() for a in arrays]), axis)
    return tuple(so_far[b:e].reshape(a.shape) for a, b, e in zip(arrays, ends, ends[1:]))


def to_windows(array, rows):
    first, second, third, rest = array.shape
    shaped = array.reshape(first // WIN, WIN, second // WIN, WIN, third // WIN, WIN, rest)
    flat = shaped.transpose(0, 2, 4, 1, 3, 5, 6).reshape(-1, TOK, rest)
    return jnp.pad(flat, ((0, 0), (0, rows - TOK), (0, 0)))


def from_windows(array, first, second, third):
    feats = array.shape[-1]
    shaped = array.reshape(first // WIN, second // WIN, third // WIN, WIN, WIN, WIN, feats)
    return shaped.transpose(0, 3, 1, 4, 2, 5, 6).reshape(first, second, third, feats)


def forward(pair, dim, axis):
    head = lax.slice_in_dim(pair, 0, SHIFT, axis=dim)
    rest = lax.slice_in_dim(pair, SHIFT, pair.shape[dim], axis=dim)
    return jnp.concatenate([rest, shifted(head, axis, -1)], dim)


def backward(field, dim, axis):
    edge = field.shape[dim] - SHIFT
    tail = lax.slice_in_dim(field, edge, field.shape[dim], axis=dim)
    rest = lax.slice_in_dim(field, 0, edge, axis=dim)
    return jnp.concatenate([shifted(tail, axis, 1), rest], dim)


def shards(inputs, d_out, gain, shift, w_qkv, b_qkv, w_proj, rel_bias):
    cells_x, cells_y, cells_z, _ = inputs.shape
    pair = jnp.stack([inputs, d_out])
    axes = ("gx", "gy", "gz")
    for d, axis in enumerate(axes):
        pair = forward(pair, d + 1, axis)
    win_x = to_windows(pair[0], ROWS)
    win_dy = to_windows(pair[1], LANES)
    dx, wq, wkv, proj, rel, rows, bq = window_call(
        win_x, win_dy, gain, shift, rel_bias, w_qkv, b_qkv, w_proj, cells_x, cells_y
    )
    field = from_windows(dx[:, :TOK], cells_x, cells_y, cells_z)
    for d, axis in enumerate(axes):
        field = backward(field, d, axis)
    sums = jnp.sum(rows, 1)
    bq = jnp.sum(bq, 1)
    weight = jnp.concatenate([wq.T, wkv[:, 0:96], wkv[:, 128:224]], 1)
    bias = jnp.concatenate([bq, sums[0], sums[1]])
    rel = rel[:HEADS, :TABLE]
    count = inputs.size // FEATS * lax.axis_size("gx") * lax.axis_size("gy") * lax.axis_size("gz")
    factor = float(count) ** -0.5
    totals = in_one((weight, bias, proj, rel, sums[2], sums[3]), axes)
    return (field,) + tuple(t * factor for t in totals)


def solution(mesh):
    placed = (P("gx", "gy", "gz", None), P("gx", "gy", "gz", None), P(), P(), P(), P(), P(), P())
    return jax.shard_map(
        shards,
        mesh=mesh,
        in_specs=placed,
        out_specs=(P("gx", "gy", "gz", None), P(), P(), P(), P(), P(), P()),
        check_vma=False,
    )
```

```python
import functools

import jax
import jax.numpy as jnp
import numpy as np
from jax import lax
from jax.experimental import pallas as pl
from jax.experimental.pallas import tpu as pltpu
from jax.sharding import PartitionSpec as P

WIN = 7
SHIFT = 3
TOK = WIN**3
ROWS = 352
LANES = 384
FEATS = 96
HEADS = 3
HDIM = 32
PLANE = 49
WIDTH = 13
TABLE = WIDTH**3
SPREAD = 2304
SQUEEZED = 768
OWN = 196
OTHER = 147
AHEAD = 3
LAG = 2
CHUNK = 56
MESH = pl.DeviceIdType.MESH
FAR = -(2.0**100)
NEVER = -1e30
LOG2E = 1.4426950408889634
SCALE = HDIM**-0.5
F32 = jnp.float32
BF16 = jnp.bfloat16


def nn(a, b):
    return lax.dot_general(a, b, (((1,), (0,)), ((), ())), preferred_element_type=F32)


def nt(a, b):
    return lax.dot_general(a, b, (((1,), (1,)), ((), ())), preferred_element_type=F32)


def token_place(count):
    p = np.arange(count)
    n = np.where(p < OWN, p // 4, (p - OWN) // 3)
    z = np.where(p < OWN, p % 4, 4 + (p - OWN) % 3)
    return n // 7, n % 7, z


def token_late(count):
    return np.stack([(place >= WIN - SHIFT).astype(np.float32) for place in token_place(count)])


def squeeze_ones():
    lane = np.arange(SQUEEZED)
    m = lane - LANES
    own = lane // 28 * 169 + lane % 28 // 4 * 13 + lane % 4
    other = m // 21 * 169 + m % 21 // 3 * 13 + 4 + m % 3
    place = np.where(lane < 364, own, np.where((m >= 0) & (m < 273), other, -1))
    return (np.arange(SPREAD)[:, None] == place[None, :]).astype(np.float32)


def key_features():
    late = token_late(ROWS)
    out = np.zeros((ROWS, 256), np.float32)
    for d in range(3):
        out[:, 96 + 2 * d] = late[d]
        out[:, 97 + 2 * d] = 1 - late[d]
    return out


def query_features():
    late = token_late(LANES)
    out = np.zeros((3, 16, LANES), np.float32)
    for d in range(3):
        out[d, 2 * d] = FAR * (1 - late[d])
        out[d, 2 * d + 1] = FAR * late[d]
    return out


def pieces(x, count):
    out = []
    for _ in range(count):
        piece = x.astype(BF16)
        out.append(piece)
        x = x - piece.astype(F32)
    return out


def expand_table(table_ref, ones_ref, bias_ref, wide_ref, flat_ref):
    for h in range(HEADS):
        row = jnp.broadcast_to(table_ref[h : h + 1, :] * LOG2E, (8, SPREAD))
        row = pltpu.roll(row, 0, 1, stride=1, stride_axis=0)
        for jy in range(WIN):
            moved = pltpu.roll(row, SPREAD - 13 * (6 - jy) - 6, 1)
            for n, piece in enumerate(pieces(moved, 3)):
                wide_ref[n, h * 56 + jy * 8 : h * 56 + jy * 8 + 8, :] = piece.astype(F32)
    total = None
    for n in range(3):
        part = nn(wide_ref[n].astype(BF16), ones_ref[...])
        total = part if total is None else total + part
    flat_ref[...] = total
    lane = lax.broadcasted_iota(jnp.int32, (56, LANES), 1)
    for h in range(HEADS):
        for jx in range(WIN):
            own = pltpu.roll(flat_ref[h * 56 : h * 56 + 56, 0:LANES], (LANES - 28 * (6 - jx)) % LANES, 1)
            other = pltpu.roll(
                flat_ref[h * 56 : h * 56 + 56, LANES:SQUEEZED], (LANES + OWN - 21 * (6 - jx)) % LANES, 1
            )
            both = jnp.where(lane < OWN, own, jnp.where(lane < TOK, other, 0.0))
            for jy in range(WIN):
                n = jx * 7 + jy
                bias_ref[h, pl.ds(4 * n, 4), :] = both[jy * 8 : jy * 8 + 4]
                bias_ref[h, pl.ds(OWN + 3 * n, 3), :] = both[jy * 8 + 4 : jy * 8 + 7]
        bias_ref[h, TOK:ROWS, :] = jnp.full((ROWS - TOK, LANES), NEVER, F32)


def fold_table(sums_ref, ones_ref, wide_ref, flat_ref, put):
    sub = lax.broadcasted_iota(jnp.int32, (8, LANES), 0)
    lane = lax.broadcasted_iota(jnp.int32, (8, LANES), 1)
    for h in range(HEADS):
        for jy in range(WIN):
            own = jnp.zeros((8, LANES), F32)
            other = jnp.zeros((8, LANES), F32)
            for jx in range(WIN):
                n = jx * 7 + jy
                low = sums_ref[h, pl.ds(4 * n, 8), :]
                high = sums_ref[h, pl.ds(OWN + 3 * n - 4, 8), :]
                block = jnp.where(sub < 4, low, high)
                own = own + pltpu.roll(jnp.where(lane < OWN, block, 0.0), 28 * (6 - jx), 1)
                rest = jnp.where((lane >= OWN) & (lane < TOK), block, 0.0)
                other = other + pltpu.roll(rest, (LANES - OWN + 21 * (6 - jx)) % LANES, 1)
            at = h * 56 + jy * 8
            flat_ref[at : at + 8, 0:LANES] = jnp.where(sub < WIN, own, 0.0)
            flat_ref[at : at + 8, LANES:SQUEEZED] = jnp.where(sub < WIN, other, 0.0)
    spread = None
    for piece in pieces(flat_ref[...], 3):
        part = nt(piece, ones_ref[...])
        spread = part if spread is None else spread + part
    wide_ref[0] = spread
    for h in range(HEADS):
        total = jnp.zeros((8, SPREAD), F32)
        for jy in range(WIN):
            block = wide_ref[0, h * 56 + jy * 8 : h * 56 + jy * 8 + 8, :]
            total = total + pltpu.roll(block, 13 * (6 - jy), 1)
        line = jnp.zeros((1, SPREAD), F32)
        for jz in range(WIN):
            line = line + pltpu.roll(total, 6 - jz, 1)[jz : jz + 1]
        for c in range(SPREAD // 128):
            put(384 + h * 18 + c, line[:, c * 128 : c * 128 + 128])


def window_at(t):
    inner = jnp.where(t < 5, t, t - 7)
    edge = t - 5
    side_x = jnp.where(edge < 4, 3, edge - 4)
    side_y = jnp.where(edge < 4, edge, 3)
    is_edge = (t >= 5) & (t < 12)
    return jnp.where(is_edge, side_x, inner // 3), jnp.where(is_edge, side_y, inner % 3)


def whole_kernel(
    x_hbm,
    dy_hbm,
    gain_ref,
    shift_ref,
    table_ref,
    ones_ref,
    w_all_ref,
    w_kv_ref,
    b_col_ref,
    b_kv_ref,
    q_feat_ref,
    w_proj_ref,
    w_qkv_ref,
    out_hbm,
    result_ref,
    bias_ref,
    acc_ref,
    e_ref,
    ds_ref,
    q_ref,
    do_ref,
    ln_ref,
    gq_ref,
    wide_ref,
    flat_ref,
    wq_ref,
    wkv_ref,
    proj_ref,
    rows_ref,
    ext_ref,
    win_ref,
    send_f_ref,
    dyb_ref,
    dx_ref,
    back_f_ref,
    out_ext_ref,
    fwd_send_ref,
    fwd_recv_ref,
    ret_send_ref,
    ret_recv_ref,
    pay_ref,
    near_ref,
    far_ref,
    load_sem,
    halo_send,
    halo_recv,
    fwd_send,
    fwd_recv,
    ret_send,
    ret_recv,
    out_sem,
    edge_send,
    edge_recv,
    near_send,
    near_recv,
    far_send,
    far_recv,
    all_send,
    all_recv,
):
    nx, ny, nz = lax.axis_size("gx"), lax.axis_size("gy"), lax.axis_size("gz")
    gx, gy, gz = lax.axis_index("gx"), lax.axis_index("gy"), lax.axis_index("gz")
    plane = nx * ny
    spot = gx * ny + gy
    cells_x, cells_y = x_hbm.shape[0], x_hbm.shape[1]
    total = (cells_x // WIN) * (cells_y // WIN)

    def peer_z(k):
        return {"gz": lax.rem(gz + k, nz)}

    def peer_xy(k):
        other = lax.rem(spot + k, plane)
        return {"gx": other // ny, "gy": lax.rem(other, ny)}

    barrier = pltpu.get_barrier_semaphore()
    for k in range(1, nz):
        pl.semaphore_signal(barrier, inc=1, device_id=peer_z(k), device_id_type=MESH)
    for k in range(1, plane):
        pl.semaphore_signal(barrier, inc=1, device_id=peer_xy(k), device_id_type=MESH)

    def load(a):
        source = (x_hbm, dy_hbm)[a]
        return pltpu.make_async_copy(
            source, ext_ref.at[a, pl.ds(0, cells_x), pl.ds(0, cells_y)], load_sem.at[a]
        )

    def halo(a, side):
        source = (x_hbm, dy_hbm)[a]
        px, py = ((1, 0), (0, 1), (1, 1))[side]
        from_x = pl.ds(0, SHIFT) if px else pl.ds(0, cells_x)
        from_y = pl.ds(0, SHIFT) if py else pl.ds(0, cells_y)
        to_x = pl.ds(cells_x, SHIFT) if px else pl.ds(0, cells_x)
        to_y = pl.ds(cells_y, SHIFT) if py else pl.ds(0, cells_y)
        return pltpu.make_async_remote_copy(
            src_ref=source.at[from_x, from_y],
            dst_ref=ext_ref.at[a, to_x, to_y],
            send_sem=halo_send.at[a, side],
            recv_sem=halo_recv.at[a, side],
            device_id={"gx": lax.rem(gx + nx - px, nx), "gy": lax.rem(gy + ny - py, ny)},
            device_id_type=MESH,
        )

    def fwd(t):
        return pltpu.make_async_remote_copy(
            src_ref=fwd_send_ref.at[t],
            dst_ref=fwd_recv_ref.at[t],
            send_sem=fwd_send.at[t],
            recv_sem=fwd_recv.at[t],
            device_id=peer_z(nz - 1),
            device_id_type=MESH,
        )

    def ret(t):
        return pltpu.make_async_remote_copy(
            src_ref=ret_send_ref.at[t],
            dst_ref=ret_recv_ref.at[t],
            send_sem=ret_send.at[t],
            recv_sem=ret_recv.at[t],
            device_id=peer_z(1),
            device_id_type=MESH,
        )

    def edge(side):
        px, py = ((1, 0), (0, 1), (1, 1))[side]
        from_x = pl.ds(cells_x, SHIFT) if px else pl.ds(SHIFT, cells_x - SHIFT)
        from_y = pl.ds(cells_y, SHIFT) if py else pl.ds(SHIFT, cells_y - SHIFT)
        to_x = pl.ds(0, SHIFT) if px else pl.ds(SHIFT, cells_x - SHIFT)
        to_y = pl.ds(0, SHIFT) if py else pl.ds(SHIFT, cells_y - SHIFT)
        return pltpu.make_async_remote_copy(
            src_ref=out_ext_ref.at[from_x, from_y],
            dst_ref=out_hbm.at[to_x, to_y],
            send_sem=edge_send.at[side],
            recv_sem=edge_recv.at[side],
            device_id={"gx": lax.rem(gx + px, nx), "gy": lax.rem(gy + py, ny)},
            device_id_type=MESH,
        )

    def store_out():
        inner_x = pl.ds(SHIFT, cells_x - SHIFT)
        inner_y = pl.ds(SHIFT, cells_y - SHIFT)
        return pltpu.make_async_copy(
            out_ext_ref.at[inner_x, inner_y], out_hbm.at[inner_x, inner_y], out_sem
        )

    def near(k):
        return pltpu.make_async_remote_copy(
            src_ref=pay_ref.at[lax.rem(gz + k, nz)],
            dst_ref=near_ref.at[gz],
            send_sem=near_send.at[k],
            recv_sem=near_recv.at[k],
            device_id=peer_z(k),
            device_id_type=MESH,
        )

    def far(k):
        return pltpu.make_async_remote_copy(
            src_ref=far_ref.at[spot],
            dst_ref=far_ref.at[spot],
            send_sem=far_send.at[k],
            recv_sem=far_recv.at[k],
            device_id=peer_xy(k),
            device_id_type=MESH,
        )

    def final(k):
        return pltpu.make_async_remote_copy(
            src_ref=result_ref.at[gz],
            dst_ref=result_ref.at[gz],
            send_sem=all_send.at[k],
            recv_sem=all_recv.at[k],
            device_id=peer_z(k),
            device_id_type=MESH,
        )

    load(0).start()
    load(1).start()
    acc_ref[...] = jnp.zeros_like(acc_ref)
    e_ref[...] = jnp.zeros_like(e_ref)
    ds_ref[...] = jnp.zeros_like(ds_ref)
    q_ref[...] = jnp.zeros_like(q_ref)
    do_ref[...] = jnp.zeros_like(do_ref)
    wq_ref[...] = jnp.zeros_like(wq_ref)
    wkv_ref[...] = jnp.zeros_like(wkv_ref)
    proj_ref[...] = jnp.zeros_like(proj_ref)
    rows_ref[...] = jnp.zeros_like(rows_ref)
    gq_ref[...] = jnp.zeros_like(gq_ref)
    ln_ref[...] = jnp.zeros_like(ln_ref)
    dyb_ref[...] = jnp.zeros_like(dyb_ref)
    send_f_ref[...] = jnp.zeros_like(send_f_ref)
    pay_ref[...] = jnp.zeros_like(pay_ref)
    for t in range(total):
        dx_ref[t, 0:8, :] = jnp.zeros((8, FEATS), F32)
        dx_ref[t, 360:368, :] = jnp.zeros((8, FEATS), F32)
    pl.semaphore_wait(barrier, nz - 1 + plane - 1)
    for a in range(2):
        for side in range(3):
            halo(a, side).start()
    load(0).wait()
    load(1).wait()

    def gather(t):
        wx, wy = window_at(t)
        for a in range(2):
            for ix in range(WIN):
                for iy in range(WIN):
                    n = ix * WIN + iy
                    tile = ext_ref[a, wx * WIN + SHIFT + ix, wy * WIN + SHIFT + iy].astype(F32)
                    win_ref[t, a, pl.ds(4 * n, 4), :] = tile[3:7]
                    send_f_ref[pl.ds(3 * n, 3), :] = tile[0:3]
            fwd_send_ref[t, a] = send_f_ref[...].astype(BF16)
        fwd(t).start()

    def first_gather(t, carry):
        gather(t)
        return carry

    lax.fori_loop(0, AHEAD, first_gather, 0)
    expand_table(table_ref, ones_ref, bias_ref, wide_ref, flat_ref)

    def compute(t):
        wx, wy = window_at(t)
        last_x = (gx == nx - 1) & (wx == cells_x // WIN - 1)
        last_y = (gy == ny - 1) & (wy == cells_y // WIN - 1)
        last_z = gz == nz - 1
        fwd(t).wait_recv()
        for a in range(2):
            win_ref[t, a, OWN:ROWS, :] = fwd_recv_ref[t, a].astype(F32)[0 : ROWS - OWN]
        x = win_ref[t, 0]
        mean = jnp.mean(x, -1, keepdims=True)
        centered = x - mean
        rstd = lax.rsqrt(jnp.mean(centered * centered, -1, keepdims=True) + 1e-05)
        xhat = centered * rstd
        ln_ref[0:ROWS, :] = (xhat * gain_ref[...] + shift_ref[...]).astype(BF16)

        across = nt(w_all_ref[...], ln_ref[...])
        q_t = ((across[0:96] + b_col_ref[0:96]) * (SCALE * LOG2E)).astype(BF16)
        k_t = (across[96:192] + b_col_ref[96:192]).astype(BF16)
        v_t = (across[192:288] + b_col_ref[192:288]).astype(BF16)
        ln_t = across[288:384].astype(BF16)
        marks = (
            q_feat_ref[0] * last_x.astype(F32)
            + q_feat_ref[1] * last_y.astype(F32)
            + q_feat_ref[2] * last_z.astype(F32)
        ).astype(BF16)
        for h in range(HEADS):
            q_ref[h * HDIM : (h + 1) * HDIM, h * LANES : (h + 1) * LANES] = q_t[h * HDIM : (h + 1) * HDIM]
            q_ref[96:112, h * LANES : (h + 1) * LANES] = marks
        kv = nn(ln_ref[0:ROWS, :], w_kv_ref[...]) + b_kv_ref[...]
        k = kv[:, 0:128].astype(BF16)
        v = kv[:, 128:256].astype(BF16)
        dyb_ref[0:ROWS, :] = win_ref[t, 1].astype(BF16)
        dy = dyb_ref[...]
        do_t = nt(w_proj_ref[...], dy)

        att = []
        for h in range(HEADS):
            inverse = []
            for c in range(3):
                at = pl.ds(h * LANES + c * 128, 128)
                s = nn(k, q_ref[:, at]) + bias_ref[h, :, pl.ds(c * 128, 128)]
                e = jnp.exp2(s - jnp.max(s, 0, keepdims=True))
                inv = 1.0 / jnp.sum(e, 0, keepdims=True)
                inverse.append(inv)
                e_ref[0:ROWS, at] = e.astype(BF16)
                do_ref[h * HDIM : (h + 1) * HDIM, at] = (
                    do_t[h * HDIM : (h + 1) * HDIM, c * 128 : c * 128 + 128] * inv
                ).astype(BF16)
                dp = nn(v, do_ref[:, at])
                ds = e * (dp - jnp.sum(e * dp, 0, keepdims=True) * inv)
                acc_ref[h, :, pl.ds(c * 128, 128)] += ds
                ds_ref[0:ROWS, at] = ds.astype(BF16)
            at = pl.ds(h * LANES, LANES)
            inverse = jnp.concatenate(inverse, 1)
            o_t = nn(v_t[h * HDIM : (h + 1) * HDIM], e_ref[:, at]) * inverse
            att.append(o_t.astype(BF16))
            gq_ref[h * HDIM : (h + 1) * HDIM, :] = nn(k_t[h * HDIM : (h + 1) * HDIM], ds_ref[:, at]) * SCALE
        att = jnp.concatenate(att, 0)
        proj_ref[...] += nn(att, dy)
        grad_v = nt(e_ref[0:ROWS, :], do_ref[...])
        grad_k = nt(ds_ref[0:ROWS, :], q_ref[0:96, :]) * (1.0 / LOG2E)
        gq = gq_ref[...]
        wq_ref[0:96, 0:96] += nn(gq[0:96].astype(BF16), ln_ref[...])
        turned = gq.T[0:ROWS, 0:96]
        grad_q = turned.astype(BF16)
        grad_v = grad_v[:, 0:96]
        k_b = grad_k.astype(BF16)
        v_b = grad_v.astype(BF16)
        wkv_ref[:, 0:96] += nn(ln_t[:, 0:ROWS], k_b)
        wkv_ref[:, 128:224] += nn(ln_t[:, 0:ROWS], v_b)
        grad_in = (
            nt(grad_q, w_qkv_ref[:, 0:96])
            + nt(k_b, w_qkv_ref[:, 128:224])
            + nt(v_b, w_qkv_ref[:, 256:352])
        )
        for n, term in enumerate((turned, grad_k, grad_v, xhat * grad_in, grad_in)):
            rows_ref[n] += jnp.sum(term.reshape(ROWS // 8, 8, 96), 0)
        dhat = grad_in * gain_ref[...]
        first = jnp.mean(dhat, -1, keepdims=True)
        second = jnp.mean(dhat * xhat, -1, keepdims=True)
        dx_ref[t, 8 : 8 + ROWS, :] = win_ref[t, 1] + rstd * (dhat - first - xhat * second)
        ret_send_ref[t] = dx_ref[t, 8 + OWN : 8 + OWN + 160, :].astype(BF16)
        ret(t).start()

    sub = lax.broadcasted_iota(jnp.int32, (8, FEATS), 0)

    def merge(t):
        wx, wy = window_at(t)
        ret(t).wait_recv()
        back_f_ref[...] = ret_recv_ref[t].astype(F32)
        for ix in range(WIN):
            for iy in range(WIN):
                n = ix * WIN + iy
                low = back_f_ref[pl.ds(3 * n, 8), :]
                high = dx_ref[t, pl.ds(5 + 4 * n, 8), :]
                tile = jnp.where(sub < SHIFT, low, high).astype(BF16)
                out_ext_ref[wx * WIN + SHIFT + ix, wy * WIN + SHIFT + iy] = tile[0:7]

    def step(t, carry):
        @pl.when(t == 5 - AHEAD)
        def _():
            for a in range(2):
                for side in range(3):
                    halo(a, side).wait_recv()

        @pl.when(t + AHEAD < total)
        def _():
            gather(t + AHEAD)

        compute(t)

        @pl.when(t >= LAG)
        def _():
            merge(t - LAG)

        return carry

    lax.fori_loop(0, total, step, 0)

    def put(row, value):
        while value.shape[0]:
            chunk, at = divmod(row, CHUNK)
            count = min(CHUNK - at, value.shape[0])
            pay_ref[chunk, at : at + count, 0 : value.shape[1]] = value[0:count]
            value = value[count:]
            row += count

    put(0, wq_ref[...].T[0:96, 0:96])
    put(96, wkv_ref[:, 0:96])
    put(192, wkv_ref[:, 128:224])
    put(288, proj_ref[...])
    for n in range(5):
        put(438 + n, jnp.sum(rows_ref[n], 0, keepdims=True))
    fold_table(acc_ref, ones_ref, wide_ref, flat_ref, put)
    for k in range(1, nz):
        near(k).start()
    near_ref[gz] = pay_ref[gz]

    def last_merge(t, carry):
        merge(t)
        return carry

    lax.fori_loop(total - LAG, total, last_merge, 0)
    store_out().start()
    for side in range(3):
        edge(side).start()
    for k in range(1, nz):
        near(k).wait_recv()
    far_ref[spot] = jnp.sum(near_ref[...], 0)
    for k in range(1, plane):
        far(k).start()
    for k in range(1, plane):
        far(k).wait_recv()
    result_ref[gz] = jnp.sum(far_ref[...], 0)
    for k in range(1, nz):
        final(k).start()
    store_out().wait()
    for side in range(3):
        edge(side).wait()
    for a in range(2):
        for side in range(3):
            halo(a, side).wait_send()

    def drain(t, carry):
        fwd(t).wait_send()
        ret(t).wait_send()
        return carry

    lax.fori_loop(0, total, drain, 0)
    for k in range(1, nz):
        near(k).wait_send()
    for k in range(1, plane):
        far(k).wait_send()
    for k in range(1, nz):
        final(k).wait()


def whole_call(inputs, d_out, gain, shift, table, w_qkv, b_qkv, w_proj):
    cells_x, cells_y, cells_z, _ = inputs.shape
    count = (cells_x // WIN) * (cells_y // WIN)
    nz, plane = lax.axis_size("gz"), lax.axis_size("gx") * lax.axis_size("gy")
    ones = jnp.asarray(squeeze_ones(), BF16)
    w_t = w_qkv.T
    w_all = jnp.concatenate([w_t, jnp.eye(96, dtype=BF16)], 0)
    gap = jnp.zeros((96, 32), BF16)
    w_k, w_v = w_qkv[:, 96:192], w_qkv[:, 192:288]
    w_kv = jnp.concatenate([w_k, gap, w_v, gap], 1)
    w_back = jnp.concatenate([w_qkv[:, 0:96], gap, w_k, gap, w_v, gap], 1)
    gap_b = jnp.zeros((32,), F32)
    b_row = jnp.concatenate([b_qkv[96:192], gap_b, b_qkv[192:288], gap_b])
    b_kv = jnp.asarray(key_features()) + b_row[None, :]
    b_col = b_qkv[:, None]
    table = jnp.pad(table, ((0, 5), (0, SPREAD - TABLE)))
    consts = (gain[None, :], shift[None, :], table, ones, w_all, w_kv, b_col, b_kv)
    consts += (jnp.asarray(query_features()), w_proj, w_back)
    outs = (
        jax.ShapeDtypeStruct(inputs.shape, BF16),
        jax.ShapeDtypeStruct((nz, CHUNK, 128), F32),
    )
    anywhere = pl.BlockSpec(memory_space=pl.ANY)
    inside = pl.BlockSpec(memory_space=pltpu.VMEM)
    dma = pltpu.SemaphoreType.DMA
    return pl.pallas_call(
        whole_kernel,
        in_specs=[anywhere] * 2 + [inside] * len(consts),
        out_specs=[anywhere, inside],
        out_shape=outs,
        scratch_shapes=[
            pltpu.VMEM((HEADS, ROWS, LANES), F32),
            pltpu.VMEM((HEADS, ROWS, LANES), F32),
            pltpu.VMEM((LANES, HEADS * LANES), BF16),
            pltpu.VMEM((LANES, HEADS * LANES), BF16),
            pltpu.VMEM((128, HEADS * LANES), BF16),
            pltpu.VMEM((128, HEADS * LANES), BF16),
            pltpu.VMEM((LANES, FEATS), BF16),
            pltpu.VMEM((128, LANES), F32),
            pltpu.VMEM((3, HEADS * 56, SPREAD), F32),
            pltpu.VMEM((HEADS * 56, SQUEEZED), F32),
            pltpu.VMEM((128, 128), F32),
            pltpu.VMEM((96, 256), F32),
            pltpu.VMEM((96, 96), F32),
            pltpu.VMEM((5, 8, 96), F32),
            pltpu.VMEM((2, cells_x + SHIFT, cells_y + SHIFT, cells_z, FEATS), BF16),
            pltpu.VMEM((count, 2, ROWS, FEATS), F32),
            pltpu.VMEM((160, FEATS), F32),
            pltpu.VMEM((LANES, FEATS), BF16),
            pltpu.VMEM((count, 368, FEATS), F32),
            pltpu.VMEM((160, FEATS), F32),
            pltpu.VMEM((cells_x + SHIFT, cells_y + SHIFT, cells_z, FEATS), BF16),
            pltpu.VMEM((count, 2, 160, FEATS), BF16),
            pltpu.VMEM((count, 2, 160, FEATS), BF16),
            pltpu.VMEM((count, 160, FEATS), BF16),
            pltpu.VMEM((count, 160, FEATS), BF16),
            pltpu.VMEM((nz, CHUNK, 128), F32),
            pltpu.VMEM((nz, CHUNK, 128), F32),
            pltpu.VMEM((plane, CHUNK, 128), F32),
            dma((2,)),
            dma((2, 3)),
            dma((2, 3)),
            dma((count,)),
            dma((count,)),
            dma((count,)),
            dma((count,)),
            dma,
            dma((3,)),
            dma((3,)),
            dma((nz,)),
            dma((nz,)),
            dma((plane,)),
            dma((plane,)),
            dma((nz,)),
            dma((nz,)),
        ],
        compiler_params=pltpu.CompilerParams(
            vmem_limit_bytes=56 << 20, collective_id=0, has_side_effects=True
        ),
    )(inputs, d_out, *consts)


def shards(inputs, d_out, gain, shift, w_qkv, b_qkv, w_proj, rel_bias):
    field, sums = whole_call(inputs, d_out, gain, shift, rel_bias, w_qkv, b_qkv, w_proj)
    count = inputs.size // FEATS * lax.axis_size("gx") * lax.axis_size("gy") * lax.axis_size("gz")
    sums = sums.reshape(-1, 128) * float(count) ** -0.5
    weight = jnp.concatenate([sums[0:96, :96], sums[96:192, :96], sums[192:288, :96]], 1)
    proj = sums[288:384, :96]
    rel = sums[384:438].reshape(HEADS, SPREAD)[:, :TABLE]
    bias = sums[438:441, :96].reshape(-1)
    return field, weight, bias, proj, rel, sums[441, :96], sums[442, :96]


def solution(mesh):
    placed = (P("gx", "gy", "gz", None), P("gx", "gy", "gz", None), P(), P(), P(), P(), P(), P())
    return jax.shard_map(
        shards,
        mesh=mesh,
        in_specs=placed,
        out_specs=(P("gx", "gy", "gz", None), P(), P(), P(), P(), P(), P()),
        check_vma=False,
    )
```

```python
import functools

import jax
import jax.numpy as jnp
import numpy as np
from jax import lax
from jax.experimental import pallas as pl
from jax.experimental.pallas import tpu as pltpu
from jax.sharding import PartitionSpec as P

WIN = 7
SHIFT = 3
TOK = WIN**3
ROWS = 352
LANES = 384
FEATS = 96
HEADS = 3
HDIM = 32
PLANE = 49
WIDTH = 13
TABLE = WIDTH**3
SPREAD = 2304
SQUEEZED = 768
OWN = 196
OTHER = 147
AHEAD = 3
LAG = 2
QUAD = 4
MESH = pl.DeviceIdType.MESH
FAR = -(2.0**100)
NEVER = -1e30
LOG2E = 1.4426950408889634
SCALE = HDIM**-0.5
F32 = jnp.float32
BF16 = jnp.bfloat16


def nn(a, b):
    return lax.dot_general(a, b, (((1,), (0,)), ((), ())), preferred_element_type=F32)


def nt(a, b):
    return lax.dot_general(a, b, (((1,), (1,)), ((), ())), preferred_element_type=F32)


def token_place(count):
    p = np.arange(count)
    n = np.where(p < OWN, p // 4, (p - OWN) // 3)
    z = np.where(p < OWN, p % 4, 4 + (p - OWN) % 3)
    return n // 7, n % 7, z


def token_late(count):
    return np.stack([(place >= WIN - SHIFT).astype(np.float32) for place in token_place(count)])


def squeeze_ones():
    lane = np.arange(SQUEEZED)
    m = lane - LANES
    own = lane // 28 * 169 + lane % 28 // 4 * 13 + lane % 4
    other = m // 21 * 169 + m % 21 // 3 * 13 + 4 + m % 3
    place = np.where(lane < 364, own, np.where((m >= 0) & (m < 273), other, -1))
    return (np.arange(SPREAD)[:, None] == place[None, :]).astype(np.float32)


def key_features():
    late = token_late(ROWS)
    out = np.zeros((ROWS, 256), np.float32)
    for d in range(3):
        out[:, 96 + 2 * d] = late[d]
        out[:, 97 + 2 * d] = 1 - late[d]
    return out


def query_features():
    late = token_late(LANES)
    out = np.zeros((3, 16, LANES), np.float32)
    for d in range(3):
        out[d, 2 * d] = FAR * (1 - late[d])
        out[d, 2 * d + 1] = FAR * late[d]
    return out


def pieces(x, count):
    out = []
    for _ in range(count):
        piece = x.astype(BF16)
        out.append(piece)
        x = x - piece.astype(F32)
    return out


def expand_table(table_ref, ones_ref, bias_ref, wide_ref, flat_ref):
    for h in range(HEADS):
        row = jnp.broadcast_to(table_ref[h : h + 1, :] * LOG2E, (8, SPREAD))
        row = pltpu.roll(row, 0, 1, stride=1, stride_axis=0)
        for jy in range(WIN):
            moved = pltpu.roll(row, SPREAD - 13 * (6 - jy) - 6, 1)
            for n, piece in enumerate(pieces(moved, 3)):
                wide_ref[n, h * 56 + jy * 8 : h * 56 + jy * 8 + 8, :] = piece.astype(F32)
    total = None
    for n in range(3):
        part = nn(wide_ref[n].astype(BF16), ones_ref[...])
        total = part if total is None else total + part
    flat_ref[...] = total
    lane = lax.broadcasted_iota(jnp.int32, (56, LANES), 1)
    for h in range(HEADS):
        for jx in range(WIN):
            own = pltpu.roll(flat_ref[h * 56 : h * 56 + 56, 0:LANES], (LANES - 28 * (6 - jx)) % LANES, 1)
            other = pltpu.roll(
                flat_ref[h * 56 : h * 56 + 56, LANES:SQUEEZED], (LANES + OWN - 21 * (6 - jx)) % LANES, 1
            )
            both = jnp.where(lane < OWN, own, jnp.where(lane < TOK, other, 0.0))
            for jy in range(WIN):
                n = jx * 7 + jy
                bias_ref[pl.ds(4 * n, 4), h * LANES : (h + 1) * LANES] = both[jy * 8 : jy * 8 + 4]
                bias_ref[pl.ds(OWN + 3 * n, 3), h * LANES : (h + 1) * LANES] = both[jy * 8 + 4 : jy * 8 + 7]
        bias_ref[TOK:ROWS, h * LANES : (h + 1) * LANES] = jnp.full((ROWS - TOK, LANES), NEVER, F32)


def fold_table(sums_ref, ones_ref, wide_ref, flat_ref, put):
    sub = lax.broadcasted_iota(jnp.int32, (8, LANES), 0)
    lane = lax.broadcasted_iota(jnp.int32, (8, LANES), 1)
    for h in range(HEADS):
        for jy in range(WIN):
            own = jnp.zeros((8, LANES), F32)
            other = jnp.zeros((8, LANES), F32)
            for jx in range(WIN):
                n = jx * 7 + jy
                low = sums_ref[pl.ds(4 * n, 8), h * LANES : (h + 1) * LANES]
                high = sums_ref[pl.ds(OWN + 3 * n - 4, 8), h * LANES : (h + 1) * LANES]
                block = jnp.where(sub < 4, low, high)
                own = own + pltpu.roll(jnp.where(lane < OWN, block, 0.0), 28 * (6 - jx), 1)
                rest = jnp.where((lane >= OWN) & (lane < TOK), block, 0.0)
                other = other + pltpu.roll(rest, (LANES - OWN + 21 * (6 - jx)) % LANES, 1)
            at = h * 56 + jy * 8
            flat_ref[at : at + 8, 0:LANES] = jnp.where(sub < WIN, own, 0.0)
            flat_ref[at : at + 8, LANES:SQUEEZED] = jnp.where(sub < WIN, other, 0.0)
    spread = None
    for piece in pieces(flat_ref[...], 3):
        part = nt(piece, ones_ref[...])
        spread = part if spread is None else spread + part
    wide_ref[0] = spread
    for h in range(HEADS):
        total = jnp.zeros((8, SPREAD), F32)
        for jy in range(WIN):
            block = wide_ref[0, h * 56 + jy * 8 : h * 56 + jy * 8 + 8, :]
            total = total + pltpu.roll(block, 13 * (6 - jy), 1)
        line = jnp.zeros((1, SPREAD), F32)
        for jz in range(WIN):
            line = line + pltpu.roll(total, 6 - jz, 1)[jz : jz + 1]
        for c in range(SPREAD // 128):
            put(384 + h * 18 + c, line[:, c * 128 : c * 128 + 128])


def window_at(t):
    inner = jnp.where(t < 5, t, t - 7)
    edge = t - 5
    side_x = jnp.where(edge < 4, 3, edge - 4)
    side_y = jnp.where(edge < 4, edge, 3)
    is_edge = (t >= 5) & (t < 12)
    return jnp.where(is_edge, side_x, inner // 3), jnp.where(is_edge, side_y, inner % 3)


def whole_kernel(
    x_hbm,
    dy_hbm,
    gain_ref,
    shift_ref,
    table_ref,
    ones_ref,
    w_raw_ref,
    b_raw_ref,
    k_feat_ref,
    q_feat_ref,
    w_proj_ref,
    out_hbm,
    result_ref,
    w_all_ref,
    w_kv_ref,
    b_col_ref,
    b_kv_ref,
    w_qkv_ref,
    wide_table_ref,
    bias_ref,
    acc_ref,
    e_ref,
    ds_ref,
    q_ref,
    do_ref,
    ln_ref,
    gq_ref,
    wide_ref,
    flat_ref,
    wq_ref,
    wkv_ref,
    proj_ref,
    rows_ref,
    ext_ref,
    win_ref,
    send_f_ref,
    dyb_ref,
    dx_ref,
    back_f_ref,
    out_ext_ref,
    fwd_send_ref,
    fwd_recv_ref,
    ret_send_ref,
    ret_recv_ref,
    pay_ref,
    near_ref,
    part_ref,
    far_ref,
    load_sem,
    halo_send,
    halo_recv,
    fwd_send,
    fwd_recv,
    ret_send,
    ret_recv,
    out_sem,
    edge_send,
    edge_recv,
    near_send,
    near_recv,
    far_send,
    far_recv,
    share_send,
    share_recv,
    all_send,
    all_recv,
):
    nx, ny, nz = lax.axis_size("gx"), lax.axis_size("gy"), lax.axis_size("gz")
    gx, gy, gz = lax.axis_index("gx"), lax.axis_index("gy"), lax.axis_index("gz")
    plane = nx * ny
    spot = gx * ny + gy
    cells_x, cells_y = x_hbm.shape[0], x_hbm.shape[1]
    total = (cells_x // WIN) * (cells_y // WIN)

    def peer_z(k):
        return {"gz": lax.rem(gz + k, nz)}

    def peer_xy(k):
        other = lax.rem(spot + k, plane)
        return {"gx": other // ny, "gy": lax.rem(other, ny)}

    barrier = pltpu.get_barrier_semaphore()
    for k in range(1, nz):
        pl.semaphore_signal(barrier, inc=1, device_id=peer_z(k), device_id_type=MESH)
    for k in range(1, plane):
        pl.semaphore_signal(barrier, inc=1, device_id=peer_xy(k), device_id_type=MESH)

    def load(a):
        source = (x_hbm, dy_hbm)[a]
        return pltpu.make_async_copy(
            source, ext_ref.at[a, pl.ds(0, cells_x), pl.ds(0, cells_y)], load_sem.at[a]
        )

    def halo(a, side):
        source = (x_hbm, dy_hbm)[a]
        px, py = ((1, 0), (0, 1), (1, 1))[side]
        from_x = pl.ds(0, SHIFT) if px else pl.ds(0, cells_x)
        from_y = pl.ds(0, SHIFT) if py else pl.ds(0, cells_y)
        to_x = pl.ds(cells_x, SHIFT) if px else pl.ds(0, cells_x)
        to_y = pl.ds(cells_y, SHIFT) if py else pl.ds(0, cells_y)
        return pltpu.make_async_remote_copy(
            src_ref=source.at[from_x, from_y],
            dst_ref=ext_ref.at[a, to_x, to_y],
            send_sem=halo_send.at[a, side],
            recv_sem=halo_recv.at[a, side],
            device_id={"gx": lax.rem(gx + nx - px, nx), "gy": lax.rem(gy + ny - py, ny)},
            device_id_type=MESH,
        )

    def fwd(t):
        return pltpu.make_async_remote_copy(
            src_ref=fwd_send_ref.at[t],
            dst_ref=fwd_recv_ref.at[t],
            send_sem=fwd_send.at[t],
            recv_sem=fwd_recv.at[t],
            device_id=peer_z(nz - 1),
            device_id_type=MESH,
        )

    def ret(t):
        return pltpu.make_async_remote_copy(
            src_ref=ret_send_ref.at[t],
            dst_ref=ret_recv_ref.at[t],
            send_sem=ret_send.at[t],
            recv_sem=ret_recv.at[t],
            device_id=peer_z(1),
            device_id_type=MESH,
        )

    def edge(side):
        px, py = ((1, 0), (0, 1), (1, 1))[side]
        from_x = pl.ds(cells_x, SHIFT) if px else pl.ds(SHIFT, cells_x - SHIFT)
        from_y = pl.ds(cells_y, SHIFT) if py else pl.ds(SHIFT, cells_y - SHIFT)
        to_x = pl.ds(0, SHIFT) if px else pl.ds(SHIFT, cells_x - SHIFT)
        to_y = pl.ds(0, SHIFT) if py else pl.ds(SHIFT, cells_y - SHIFT)
        return pltpu.make_async_remote_copy(
            src_ref=out_ext_ref.at[from_x, from_y],
            dst_ref=out_hbm.at[to_x, to_y],
            send_sem=edge_send.at[side],
            recv_sem=edge_recv.at[side],
            device_id={"gx": lax.rem(gx + px, nx), "gy": lax.rem(gy + py, ny)},
            device_id_type=MESH,
        )

    def store_out():
        inner_x = pl.ds(SHIFT, cells_x - SHIFT)
        inner_y = pl.ds(SHIFT, cells_y - SHIFT)
        return pltpu.make_async_copy(
            out_ext_ref.at[inner_x, inner_y], out_hbm.at[inner_x, inner_y], out_sem
        )

    def near(k):
        return pltpu.make_async_remote_copy(
            src_ref=pay_ref.at[lax.rem(gz + k, nz)],
            dst_ref=near_ref.at[gz],
            send_sem=near_send.at[k],
            recv_sem=near_recv.at[k],
            device_id=peer_z(k),
            device_id_type=MESH,
        )

    def far(k):
        return pltpu.make_async_remote_copy(
            src_ref=part_ref.at[lax.rem(spot + k, plane)],
            dst_ref=far_ref.at[spot],
            send_sem=far_send.at[k],
            recv_sem=far_recv.at[k],
            device_id=peer_xy(k),
            device_id_type=MESH,
        )

    def share(k):
        return pltpu.make_async_remote_copy(
            src_ref=result_ref.at[gz, spot],
            dst_ref=result_ref.at[gz, spot],
            send_sem=share_send.at[k],
            recv_sem=share_recv.at[k],
            device_id=peer_xy(k),
            device_id_type=MESH,
        )

    def final(k):
        return pltpu.make_async_remote_copy(
            src_ref=result_ref.at[gz],
            dst_ref=result_ref.at[gz],
            send_sem=all_send.at[k],
            recv_sem=all_recv.at[k],
            device_id=peer_z(k),
            device_id_type=MESH,
        )

    load(0).start()
    load(1).start()
    acc_ref[...] = jnp.zeros_like(acc_ref)
    e_ref[...] = jnp.zeros_like(e_ref)
    ds_ref[...] = jnp.zeros_like(ds_ref)
    q_ref[...] = jnp.zeros_like(q_ref)
    do_ref[...] = jnp.zeros_like(do_ref)
    wq_ref[...] = jnp.zeros_like(wq_ref)
    wkv_ref[...] = jnp.zeros_like(wkv_ref)
    proj_ref[...] = jnp.zeros_like(proj_ref)
    rows_ref[...] = jnp.zeros_like(rows_ref)
    gq_ref[...] = jnp.zeros_like(gq_ref)
    ln_ref[...] = jnp.zeros_like(ln_ref)
    dyb_ref[...] = jnp.zeros_like(dyb_ref)
    send_f_ref[...] = jnp.zeros_like(send_f_ref)
    pay_ref[...] = jnp.zeros_like(pay_ref)
    for t in range(total):
        dx_ref[t, 0:8, :] = jnp.zeros((8, FEATS), F32)
        dx_ref[t, 360:368, :] = jnp.zeros((8, FEATS), F32)
    gq_ref[0:96, 0:288] = w_raw_ref[...].astype(F32)
    wide_w = gq_ref[...]
    lane = lax.broadcasted_iota(jnp.int32, (96, 128), 1)
    w_all_ref[0:288, :] = wide_w.T[0:288, 0:96].astype(BF16)
    eye = lax.broadcasted_iota(jnp.int32, (96, 96), 0) == lax.broadcasted_iota(jnp.int32, (96, 96), 1)
    w_all_ref[288:384, :] = eye.astype(F32).astype(BF16)
    turns = [wide_w if n == 0 else pltpu.roll(wide_w, LANES - 96 * n, 1) for n in range(3)]
    for n in range(3):
        piece = jnp.where(lane < FEATS, turns[n][0:96, 0:128], 0.0).astype(BF16)
        w_qkv_ref[:, n * 128 : n * 128 + 128] = piece
        if n:
            w_kv_ref[:, n * 128 - 128 : n * 128] = piece
    gq_ref[...] = jnp.zeros_like(gq_ref)
    gq_ref[:, 0:288] = jnp.broadcast_to(b_raw_ref[...], (128, 288))
    wide_b = gq_ref[...]
    b_col_ref[...] = wide_b.T
    for n in (1, 2):
        piece = jnp.where(lane[0:1] < FEATS, pltpu.roll(wide_b, LANES - 96 * n, 1)[0:1, 0:128], 0.0)
        b_kv_ref[:, n * 128 - 128 : n * 128] = k_feat_ref[:, n * 128 - 128 : n * 128] + piece
    gq_ref[...] = jnp.zeros_like(gq_ref)
    wide_table_ref[...] = jnp.zeros_like(wide_table_ref)
    wide_table_ref[0:HEADS, 0:TABLE] = table_ref[...]
    pl.semaphore_wait(barrier, nz - 1 + plane - 1)
    for a in range(2):
        for side in range(3):
            halo(a, side).start()
    load(0).wait()
    load(1).wait()

    def gather(t):
        wx, wy = window_at(t)
        for a in range(2):
            for ix in range(WIN):
                for iy in range(WIN):
                    n = ix * WIN + iy
                    tile = ext_ref[a, wx * WIN + SHIFT + ix, wy * WIN + SHIFT + iy].astype(F32)
                    win_ref[t, a, pl.ds(4 * n, 4), :] = tile[3:7]
                    send_f_ref[pl.ds(3 * n, 3), :] = tile[0:3]
            fwd_send_ref[t, a] = send_f_ref[...].astype(BF16)
        fwd(t).start()

    def first_gather(t, carry):
        gather(t)
        return carry

    lax.fori_loop(0, AHEAD, first_gather, 0)
    expand_table(wide_table_ref, ones_ref, bias_ref, wide_ref, flat_ref)

    def compute(t):
        wx, wy = window_at(t)
        last_x = (gx == nx - 1) & (wx == cells_x // WIN - 1)
        last_y = (gy == ny - 1) & (wy == cells_y // WIN - 1)
        last_z = gz == nz - 1
        fwd(t).wait_recv()
        for a in range(2):
            win_ref[t, a, OWN:ROWS, :] = fwd_recv_ref[t, a].astype(F32)[0 : ROWS - OWN]
        x = win_ref[t, 0]
        mean = jnp.mean(x, -1, keepdims=True)
        centered = x - mean
        rstd = lax.rsqrt(jnp.mean(centered * centered, -1, keepdims=True) + 1e-05)
        xhat = centered * rstd
        ln_ref[0:ROWS, :] = (xhat * gain_ref[...] + shift_ref[...]).astype(BF16)

        across = nt(w_all_ref[...], ln_ref[...])
        q_t = ((across[0:96] + b_col_ref[0:96, 0:1]) * (SCALE * LOG2E)).astype(BF16)
        k_t = (across[96:192] + b_col_ref[96:192, 0:1]).astype(BF16)
        v_t = (across[192:288] + b_col_ref[192:288, 0:1]).astype(BF16)
        ln_t = across[288:384].astype(BF16)
        marks = (
            q_feat_ref[0] * last_x.astype(F32)
            + q_feat_ref[1] * last_y.astype(F32)
            + q_feat_ref[2] * last_z.astype(F32)
        ).astype(BF16)
        for h in range(HEADS):
            q_ref[h * HDIM : (h + 1) * HDIM, h * LANES : (h + 1) * LANES] = q_t[h * HDIM : (h + 1) * HDIM]
            q_ref[96:112, h * LANES : (h + 1) * LANES] = marks
        kv = nn(ln_ref[0:ROWS, :], w_kv_ref[...]) + b_kv_ref[...]
        k = kv[:, 0:128].astype(BF16)
        v = kv[:, 128:256].astype(BF16)
        dyb_ref[0:ROWS, :] = win_ref[t, 1].astype(BF16)
        dy = dyb_ref[...]
        do_t = nt(w_proj_ref[...], dy)

        for h in range(HEADS):
            do_ref[h * HDIM : (h + 1) * HDIM, h * LANES : (h + 1) * LANES] = do_t[h * HDIM : (h + 1) * HDIM].astype(BF16)
        for u in range(0, HEADS * LANES, 256):
            at = pl.ds(u, min(256, HEADS * LANES - u))
            s = nn(k, q_ref[:, at]) + bias_ref[:, at]
            dp = nn(v, do_ref[:, at])
            e = jnp.exp2(s - jnp.max(s, 0, keepdims=True))
            e = e * (1.0 / jnp.sum(e, 0, keepdims=True))
            e_ref[0:ROWS, at] = e.astype(BF16)
            ds = e * (dp - jnp.sum(e * dp, 0, keepdims=True))
            acc_ref[:, at] += ds
            ds_ref[0:ROWS, at] = ds.astype(BF16)
        att = []
        for h in range(HEADS):
            at = pl.ds(h * LANES, LANES)
            att.append(nn(v_t[h * HDIM : (h + 1) * HDIM], e_ref[:, at]).astype(BF16))
            gq_ref[h * HDIM : (h + 1) * HDIM, :] = nn(k_t[h * HDIM : (h + 1) * HDIM], ds_ref[:, at]) * SCALE
        att = jnp.concatenate(att, 0)
        proj_ref[...] += nn(att, dy)
        grad_v = nt(e_ref[0:ROWS, :], do_ref[...])
        grad_k = nt(ds_ref[0:ROWS, :], q_ref[0:96, :]) * (1.0 / LOG2E)
        gq = gq_ref[...]
        wq_ref[0:96, 0:96] += nn(gq[0:96].astype(BF16), ln_ref[...])
        turned = gq.T[0:ROWS, 0:96]
        grad_q = turned.astype(BF16)
        grad_v = grad_v[:, 0:96]
        k_b = grad_k.astype(BF16)
        v_b = grad_v.astype(BF16)
        wkv_ref[:, 0:96] += nn(ln_t[:, 0:ROWS], k_b)
        wkv_ref[:, 128:224] += nn(ln_t[:, 0:ROWS], v_b)
        grad_in = (
            nt(grad_q, w_qkv_ref[:, 0:96])
            + nt(k_b, w_qkv_ref[:, 128:224])
            + nt(v_b, w_qkv_ref[:, 256:352])
        )
        for n, term in enumerate((turned, grad_k, grad_v, xhat * grad_in, grad_in)):
            rows_ref[n] += jnp.sum(term.reshape(ROWS // 8, 8, 96), 0)
        dhat = grad_in * gain_ref[...]
        first = jnp.mean(dhat, -1, keepdims=True)
        second = jnp.mean(dhat * xhat, -1, keepdims=True)
        dx_ref[t, 8 : 8 + ROWS, :] = win_ref[t, 1] + rstd * (dhat - first - xhat * second)
        ret_send_ref[t] = dx_ref[t, 8 + OWN : 8 + OWN + 160, :].astype(BF16)
        ret(t).start()

    sub = lax.broadcasted_iota(jnp.int32, (8, FEATS), 0)

    def merge(t):
        wx, wy = window_at(t)
        ret(t).wait_recv()
        back_f_ref[...] = ret_recv_ref[t].astype(F32)
        for ix in range(WIN):
            for iy in range(WIN):
                n = ix * WIN + iy
                low = back_f_ref[pl.ds(3 * n, 8), :]
                high = dx_ref[t, pl.ds(5 + 4 * n, 8), :]
                tile = jnp.where(sub < SHIFT, low, high).astype(BF16)
                out_ext_ref[wx * WIN + SHIFT + ix, wy * WIN + SHIFT + iy] = tile[0:7]

    def step(t, carry):
        @pl.when(t == 5 - AHEAD)
        def _():
            for a in range(2):
                for side in range(3):
                    halo(a, side).wait_recv()

        @pl.when(t + AHEAD < total)
        def _():
            gather(t + AHEAD)

        compute(t)

        @pl.when(t >= LAG)
        def _():
            merge(t - LAG)

        return carry

    lax.fori_loop(0, total, step, 0)

    block = plane * QUAD

    def put(row, value):
        while value.shape[0]:
            at = row % QUAD
            count = min(QUAD - at, value.shape[0])
            pay_ref[row // block, row % block // QUAD, at : at + count, 0 : value.shape[1]] = value[0:count]
            value = value[count:]
            row += count

    table_block = 384 // block
    put(0, wq_ref[...].T[0:96, 0:96])
    put(96, wkv_ref[:, 0:96])
    put(192, wkv_ref[:, 128:224])
    put(288, proj_ref[...])
    for k in range(1, nz):
        @pl.when(lax.rem(gz + k, nz) != table_block)
        def _():
            near(k).start()

    def last_merge(t, carry):
        merge(t)
        return carry

    lax.fori_loop(total - LAG, total, last_merge, 0)
    store_out().start()
    for side in range(3):
        edge(side).start()
    for n in range(5):
        put(438 + n, jnp.sum(rows_ref[n], 0, keepdims=True))
    fold_table(acc_ref, ones_ref, wide_ref, flat_ref, put)
    for k in range(1, nz):
        @pl.when(lax.rem(gz + k, nz) == table_block)
        def _():
            near(k).start()
    near_ref[gz] = pay_ref[gz]
    for k in range(1, nz):
        near(k).wait_recv()
    part_ref[...] = jnp.sum(near_ref[...], 0)
    for k in range(1, plane):
        far(k).start()
    far_ref[spot] = part_ref[spot]
    for k in range(1, plane):
        far(k).wait_recv()
    result_ref[gz, spot] = jnp.sum(far_ref[...], 0)
    for k in range(1, plane):
        share(k).start()
    for k in range(1, plane):
        share(k).wait_recv()
    for k in range(1, nz):
        final(k).start()
    store_out().wait()
    for side in range(3):
        edge(side).wait()
    for a in range(2):
        for side in range(3):
            halo(a, side).wait_send()

    def drain(t, carry):
        fwd(t).wait_send()
        ret(t).wait_send()
        return carry

    lax.fori_loop(0, total, drain, 0)
    for k in range(1, nz):
        near(k).wait_send()
    for k in range(1, plane):
        far(k).wait_send()
        share(k).wait_send()
    for k in range(1, nz):
        final(k).wait()


def whole_call(inputs, d_out, gain, shift, table, w_qkv, b_qkv, w_proj):
    cells_x, cells_y, cells_z, _ = inputs.shape
    count = (cells_x // WIN) * (cells_y // WIN)
    nz, plane = lax.axis_size("gz"), lax.axis_size("gx") * lax.axis_size("gy")
    ones = jnp.asarray(squeeze_ones(), BF16)
    consts = (gain[None, :], shift[None, :], table, ones, w_qkv, b_qkv[None, :])
    consts += (jnp.asarray(key_features()), jnp.asarray(query_features()), w_proj)
    outs = (
        jax.ShapeDtypeStruct(inputs.shape, BF16),
        jax.ShapeDtypeStruct((nz, plane, QUAD, 128), F32),
    )
    anywhere = pl.BlockSpec(memory_space=pl.ANY)
    inside = pl.BlockSpec(memory_space=pltpu.VMEM)
    dma = pltpu.SemaphoreType.DMA
    return pl.pallas_call(
        whole_kernel,
        in_specs=[anywhere] * 2 + [inside] * len(consts),
        out_specs=[anywhere, inside],
        out_shape=outs,
        scratch_shapes=[
            pltpu.VMEM((LANES, FEATS), BF16),
            pltpu.VMEM((96, 256), BF16),
            pltpu.VMEM((LANES, 128), F32),
            pltpu.VMEM((ROWS, 256), F32),
            pltpu.VMEM((96, LANES), BF16),
            pltpu.VMEM((8, SPREAD), F32),
            pltpu.VMEM((ROWS, HEADS * LANES), F32),
            pltpu.VMEM((ROWS, HEADS * LANES), F32),
            pltpu.VMEM((LANES, HEADS * LANES), BF16),
            pltpu.VMEM((LANES, HEADS * LANES), BF16),
            pltpu.VMEM((128, HEADS * LANES), BF16),
            pltpu.VMEM((128, HEADS * LANES), BF16),
            pltpu.VMEM((LANES, FEATS), BF16),
            pltpu.VMEM((128, LANES), F32),
            pltpu.VMEM((3, HEADS * 56, SPREAD), F32),
            pltpu.VMEM((HEADS * 56, SQUEEZED), F32),
            pltpu.VMEM((128, 128), F32),
            pltpu.VMEM((96, 256), F32),
            pltpu.VMEM((96, 96), F32),
            pltpu.VMEM((5, 8, 96), F32),
            pltpu.VMEM((2, cells_x + SHIFT, cells_y + SHIFT, cells_z, FEATS), BF16),
            pltpu.VMEM((count, 2, ROWS, FEATS), F32),
            pltpu.VMEM((160, FEATS), F32),
            pltpu.VMEM((LANES, FEATS), BF16),
            pltpu.VMEM((count, 368, FEATS), F32),
            pltpu.VMEM((160, FEATS), F32),
            pltpu.VMEM((cells_x + SHIFT, cells_y + SHIFT, cells_z, FEATS), BF16),
            pltpu.VMEM((count, 2, 160, FEATS), BF16),
            pltpu.VMEM((count, 2, 160, FEATS), BF16),
            pltpu.VMEM((count, 160, FEATS), BF16),
            pltpu.VMEM((count, 160, FEATS), BF16),
            pltpu.VMEM((nz, plane, QUAD, 128), F32),
            pltpu.VMEM((nz, plane, QUAD, 128), F32),
            pltpu.VMEM((plane, QUAD, 128), F32),
            pltpu.VMEM((plane, QUAD, 128), F32),
            dma((2,)),
            dma((2, 3)),
            dma((2, 3)),
            dma((count,)),
            dma((count,)),
            dma((count,)),
            dma((count,)),
            dma,
            dma((3,)),
            dma((3,)),
            dma((nz,)),
            dma((nz,)),
            dma((plane,)),
            dma((plane,)),
            dma((plane,)),
            dma((plane,)),
            dma((nz,)),
            dma((nz,)),
        ],
        compiler_params=pltpu.CompilerParams(
            vmem_limit_bytes=56 << 20, collective_id=0, has_side_effects=True
        ),
    )(inputs, d_out, *consts)


def shards(inputs, d_out, gain, shift, w_qkv, b_qkv, w_proj, rel_bias):
    field, sums = whole_call(inputs, d_out, gain, shift, rel_bias, w_qkv, b_qkv, w_proj)
    count = inputs.size // FEATS * lax.axis_size("gx") * lax.axis_size("gy") * lax.axis_size("gz")
    sums = sums.reshape(-1, 128) * float(count) ** -0.5
    weight = jnp.concatenate([sums[0:96, :96], sums[96:192, :96], sums[192:288, :96]], 1)
    proj = sums[288:384, :96]
    rel = sums[384:438].reshape(HEADS, SPREAD)[:, :TABLE]
    bias = sums[438:441, :96].reshape(-1)
    return field, weight, bias, proj, rel, sums[441, :96], sums[442, :96]


def solution(mesh):
    placed = (P("gx", "gy", "gz", None), P("gx", "gy", "gz", None), P(), P(), P(), P(), P(), P())
    return jax.shard_map(
        shards,
        mesh=mesh,
        in_specs=placed,
        out_specs=(P("gx", "gy", "gz", None), P(), P(), P(), P(), P(), P()),
        check_vma=False,
    )
```

```python
import functools

import jax
import jax.numpy as jnp
import numpy as np
from jax import lax
from jax.experimental import pallas as pl
from jax.experimental.pallas import tpu as pltpu
from jax.sharding import PartitionSpec as P

WIN = 7
SHIFT = 3
TOK = WIN**3
ROWS = 352
LANES = 384
FEATS = 96
HEADS = 3
HDIM = 32
PLANE = 49
WIDTH = 13
TABLE = WIDTH**3
SPREAD = 2304
SQUEEZED = 768
OWN = 196
OTHER = 147
AHEAD = 4
LAG = 3
QUAD = 4
MESH = pl.DeviceIdType.MESH
FAR = -(2.0**100)
NEVER = -1e30
LOG2E = 1.4426950408889634
SCALE = HDIM**-0.5
F32 = jnp.float32
BF16 = jnp.bfloat16


def nn(a, b):
    return lax.dot_general(a, b, (((1,), (0,)), ((), ())), preferred_element_type=F32)


def nt(a, b):
    return lax.dot_general(a, b, (((1,), (1,)), ((), ())), preferred_element_type=F32)


def token_place(count):
    p = np.arange(count)
    n = np.where(p < OWN, p // 4, (p - OWN) // 3)
    z = np.where(p < OWN, p % 4, 4 + (p - OWN) % 3)
    return n // 7, n % 7, z


def token_late(count):
    return np.stack([(place >= WIN - SHIFT).astype(np.float32) for place in token_place(count)])


def squeeze_ones():
    lane = np.arange(SQUEEZED)
    m = lane - LANES
    own = lane // 28 * 169 + lane % 28 // 4 * 13 + lane % 4
    other = m // 21 * 169 + m % 21 // 3 * 13 + 4 + m % 3
    place = np.where(lane < 364, own, np.where((m >= 0) & (m < 273), other, -1))
    return (np.arange(SPREAD)[:, None] == place[None, :]).astype(np.float32)


def key_features():
    late = token_late(ROWS)
    out = np.zeros((ROWS, 256), np.float32)
    for d in range(3):
        out[:, 96 + 2 * d] = late[d]
        out[:, 97 + 2 * d] = 1 - late[d]
    return out


def query_features():
    late = token_late(LANES)
    out = np.zeros((3, 16, LANES), np.float32)
    for d in range(3):
        out[d, 2 * d] = FAR * (1 - late[d])
        out[d, 2 * d + 1] = FAR * late[d]
    return out


def pieces(x, count):
    out = []
    for _ in range(count):
        piece = x.astype(BF16)
        out.append(piece)
        x = x - piece.astype(F32)
    return out


def expand_table(table_ref, ones_ref, bias_ref, wide_ref, flat_ref):
    for h in range(HEADS):
        row = jnp.broadcast_to(table_ref[h : h + 1, :] * LOG2E, (8, SPREAD))
        row = pltpu.roll(row, 0, 1, stride=1, stride_axis=0)
        for jy in range(WIN):
            moved = pltpu.roll(row, SPREAD - 13 * (6 - jy) - 6, 1)
            for n, piece in enumerate(pieces(moved, 3)):
                wide_ref[n, h * 56 + jy * 8 : h * 56 + jy * 8 + 8, :] = piece.astype(F32)
    total = None
    for n in range(3):
        part = nn(wide_ref[n].astype(BF16), ones_ref[...])
        total = part if total is None else total + part
    flat_ref[...] = total
    lane = lax.broadcasted_iota(jnp.int32, (56, LANES), 1)
    for h in range(HEADS):
        for jx in range(WIN):
            own = pltpu.roll(flat_ref[h * 56 : h * 56 + 56, 0:LANES], (LANES - 28 * (6 - jx)) % LANES, 1)
            other = pltpu.roll(
                flat_ref[h * 56 : h * 56 + 56, LANES:SQUEEZED], (LANES + OWN - 21 * (6 - jx)) % LANES, 1
            )
            both = jnp.where(lane < OWN, own, jnp.where(lane < TOK, other, 0.0))
            for jy in range(WIN):
                n = jx * 7 + jy
                bias_ref[pl.ds(4 * n, 4), h * LANES : (h + 1) * LANES] = both[jy * 8 : jy * 8 + 4]
                bias_ref[pl.ds(OWN + 3 * n, 3), h * LANES : (h + 1) * LANES] = both[jy * 8 + 4 : jy * 8 + 7]
        bias_ref[TOK:ROWS, h * LANES : (h + 1) * LANES] = jnp.full((ROWS - TOK, LANES), NEVER, F32)


def fold_table(sums_ref, ones_ref, wide_ref, flat_ref, put):
    sub = lax.broadcasted_iota(jnp.int32, (8, LANES), 0)
    lane = lax.broadcasted_iota(jnp.int32, (8, LANES), 1)
    for h in range(HEADS):
        for jy in range(WIN):
            own = jnp.zeros((8, LANES), F32)
            other = jnp.zeros((8, LANES), F32)
            for jx in range(WIN):
                n = jx * 7 + jy
                low = sums_ref[pl.ds(4 * n, 8), h * LANES : (h + 1) * LANES]
                high = sums_ref[pl.ds(OWN + 3 * n - 4, 8), h * LANES : (h + 1) * LANES]
                block = jnp.where(sub < 4, low, high)
                own = own + pltpu.roll(jnp.where(lane < OWN, block, 0.0), 28 * (6 - jx), 1)
                rest = jnp.where((lane >= OWN) & (lane < TOK), block, 0.0)
                other = other + pltpu.roll(rest, (LANES - OWN + 21 * (6 - jx)) % LANES, 1)
            at = h * 56 + jy * 8
            flat_ref[at : at + 8, 0:LANES] = jnp.where(sub < WIN, own, 0.0)
            flat_ref[at : at + 8, LANES:SQUEEZED] = jnp.where(sub < WIN, other, 0.0)
    spread = None
    for piece in pieces(flat_ref[...], 3):
        part = nt(piece, ones_ref[...])
        spread = part if spread is None else spread + part
    wide_ref[0] = spread
    for h in range(HEADS):
        total = jnp.zeros((8, SPREAD), F32)
        for jy in range(WIN):
            block = wide_ref[0, h * 56 + jy * 8 : h * 56 + jy * 8 + 8, :]
            total = total + pltpu.roll(block, 13 * (6 - jy), 1)
        line = jnp.zeros((1, SPREAD), F32)
        for jz in range(WIN):
            line = line + pltpu.roll(total, 6 - jz, 1)[jz : jz + 1]
        for c in range(SPREAD // 128):
            put(384 + h * 18 + c, line[:, c * 128 : c * 128 + 128])


def window_at(t):
    inner = jnp.where(t < 5, t, t - 7)
    edge = t - 5
    side_x = jnp.where(edge < 4, 3, edge - 4)
    side_y = jnp.where(edge < 4, edge, 3)
    is_edge = (t >= 5) & (t < 12)
    return jnp.where(is_edge, side_x, inner // 3), jnp.where(is_edge, side_y, inner % 3)


def whole_kernel(
    x_hbm,
    dy_hbm,
    gain_ref,
    shift_ref,
    table_ref,
    ones_ref,
    w_raw_ref,
    b_raw_ref,
    k_feat_ref,
    q_feat_ref,
    w_proj_ref,
    out_hbm,
    result_ref,
    w_all_ref,
    w_kv_ref,
    b_col_ref,
    b_kv_ref,
    w_qkv_ref,
    wide_table_ref,
    bias_ref,
    acc_ref,
    e_ref,
    ds_ref,
    q_ref,
    do_ref,
    ln_ref,
    gq_ref,
    wide_ref,
    flat_ref,
    wq_ref,
    wkv_ref,
    proj_ref,
    rows_ref,
    ext_ref,
    win_ref,
    send_f_ref,
    dyb_ref,
    dx_ref,
    back_f_ref,
    out_ext_ref,
    fwd_send_ref,
    fwd_recv_ref,
    ret_send_ref,
    ret_recv_ref,
    pay_ref,
    near_ref,
    part_ref,
    far_ref,
    load_sem,
    halo_send,
    halo_recv,
    fwd_send,
    fwd_recv,
    ret_send,
    ret_recv,
    out_sem,
    edge_send,
    edge_recv,
    near_send,
    near_recv,
    far_send,
    far_recv,
    share_send,
    share_recv,
    all_send,
    all_recv,
):
    nx, ny, nz = lax.axis_size("gx"), lax.axis_size("gy"), lax.axis_size("gz")
    gx, gy, gz = lax.axis_index("gx"), lax.axis_index("gy"), lax.axis_index("gz")
    plane = nx * ny
    spot = gx * ny + gy
    cells_x, cells_y = x_hbm.shape[0], x_hbm.shape[1]
    total = (cells_x // WIN) * (cells_y // WIN)

    def peer_z(k):
        return {"gz": lax.rem(gz + k, nz)}

    def peer_xy(k):
        other = lax.rem(spot + k, plane)
        return {"gx": other // ny, "gy": lax.rem(other, ny)}

    barrier = pltpu.get_barrier_semaphore()
    for k in range(1, nz):
        pl.semaphore_signal(barrier, inc=1, device_id=peer_z(k), device_id_type=MESH)
    for k in range(1, plane):
        pl.semaphore_signal(barrier, inc=1, device_id=peer_xy(k), device_id_type=MESH)

    def load(a):
        source = (x_hbm, dy_hbm)[a]
        return pltpu.make_async_copy(
            source, ext_ref.at[a, pl.ds(0, cells_x), pl.ds(0, cells_y)], load_sem.at[a]
        )

    def halo(a, side):
        source = (x_hbm, dy_hbm)[a]
        px, py = ((1, 0), (0, 1), (1, 1))[side]
        from_x = pl.ds(0, SHIFT) if px else pl.ds(0, cells_x)
        from_y = pl.ds(0, SHIFT) if py else pl.ds(0, cells_y)
        to_x = pl.ds(cells_x, SHIFT) if px else pl.ds(0, cells_x)
        to_y = pl.ds(cells_y, SHIFT) if py else pl.ds(0, cells_y)
        return pltpu.make_async_remote_copy(
            src_ref=source.at[from_x, from_y],
            dst_ref=ext_ref.at[a, to_x, to_y],
            send_sem=halo_send.at[a, side],
            recv_sem=halo_recv.at[a, side],
            device_id={"gx": lax.rem(gx + nx - px, nx), "gy": lax.rem(gy + ny - py, ny)},
            device_id_type=MESH,
        )

    def fwd(t):
        return pltpu.make_async_remote_copy(
            src_ref=fwd_send_ref.at[t],
            dst_ref=fwd_recv_ref.at[t],
            send_sem=fwd_send,
            recv_sem=fwd_recv.at[t],
            device_id=peer_z(nz - 1),
            device_id_type=MESH,
        )

    def ret(t):
        return pltpu.make_async_remote_copy(
            src_ref=ret_send_ref.at[t],
            dst_ref=ret_recv_ref.at[t],
            send_sem=ret_send,
            recv_sem=ret_recv.at[t],
            device_id=peer_z(1),
            device_id_type=MESH,
        )

    def edge(side):
        px, py = ((1, 0), (0, 1), (1, 1))[side]
        from_x = pl.ds(cells_x, SHIFT) if px else pl.ds(SHIFT, cells_x - SHIFT)
        from_y = pl.ds(cells_y, SHIFT) if py else pl.ds(SHIFT, cells_y - SHIFT)
        to_x = pl.ds(0, SHIFT) if px else pl.ds(SHIFT, cells_x - SHIFT)
        to_y = pl.ds(0, SHIFT) if py else pl.ds(SHIFT, cells_y - SHIFT)
        return pltpu.make_async_remote_copy(
            src_ref=out_ext_ref.at[from_x, from_y],
            dst_ref=out_hbm.at[to_x, to_y],
            send_sem=edge_send.at[side],
            recv_sem=edge_recv.at[side],
            device_id={"gx": lax.rem(gx + px, nx), "gy": lax.rem(gy + py, ny)},
            device_id_type=MESH,
        )

    def store_out(n):
        first, last = ((SHIFT, 17), (24, cells_x), (17, 24))[n]
        rows = pl.ds(first, last - first)
        inner_y = pl.ds(SHIFT, cells_y - SHIFT)
        return pltpu.make_async_copy(out_ext_ref.at[rows, inner_y], out_hbm.at[rows, inner_y], out_sem.at[n])

    def wait_bytes(like, sem):
        pltpu.make_async_copy(like, like, sem).wait()

    def near(k):
        return pltpu.make_async_remote_copy(
            src_ref=pay_ref.at[lax.rem(gz + k, nz)],
            dst_ref=near_ref.at[gz],
            send_sem=near_send,
            recv_sem=near_recv,
            device_id=peer_z(k),
            device_id_type=MESH,
        )

    def far(k):
        return pltpu.make_async_remote_copy(
            src_ref=part_ref.at[lax.rem(spot + k, plane)],
            dst_ref=far_ref.at[spot],
            send_sem=far_send,
            recv_sem=far_recv,
            device_id=peer_xy(k),
            device_id_type=MESH,
        )

    def share(k):
        return pltpu.make_async_remote_copy(
            src_ref=result_ref.at[gz, spot],
            dst_ref=result_ref.at[gz, spot],
            send_sem=share_send,
            recv_sem=share_recv,
            device_id=peer_xy(k),
            device_id_type=MESH,
        )

    def final(k):
        return pltpu.make_async_remote_copy(
            src_ref=result_ref.at[gz],
            dst_ref=result_ref.at[gz],
            send_sem=all_send,
            recv_sem=all_recv,
            device_id=peer_z(k),
            device_id_type=MESH,
        )

    load(0).start()
    load(1).start()
    acc_ref[...] = jnp.zeros_like(acc_ref)
    e_ref[...] = jnp.zeros_like(e_ref)
    ds_ref[...] = jnp.zeros_like(ds_ref)
    q_ref[...] = jnp.zeros_like(q_ref)
    do_ref[...] = jnp.zeros_like(do_ref)
    wq_ref[...] = jnp.zeros_like(wq_ref)
    wkv_ref[...] = jnp.zeros_like(wkv_ref)
    proj_ref[...] = jnp.zeros_like(proj_ref)
    rows_ref[...] = jnp.zeros_like(rows_ref)
    gq_ref[...] = jnp.zeros_like(gq_ref)
    ln_ref[...] = jnp.zeros_like(ln_ref)
    dyb_ref[...] = jnp.zeros_like(dyb_ref)
    send_f_ref[...] = jnp.zeros_like(send_f_ref)
    pay_ref[...] = jnp.zeros_like(pay_ref)
    for t in range(total):
        dx_ref[t, 0:8, :] = jnp.zeros((8, FEATS), F32)
        dx_ref[t, 360:368, :] = jnp.zeros((8, FEATS), F32)
    gq_ref[0:96, 0:288] = w_raw_ref[...].astype(F32)
    wide_w = gq_ref[...]
    lane = lax.broadcasted_iota(jnp.int32, (96, 128), 1)
    w_all_ref[0:288, :] = wide_w.T[0:288, 0:96].astype(BF16)
    eye = lax.broadcasted_iota(jnp.int32, (96, 96), 0) == lax.broadcasted_iota(jnp.int32, (96, 96), 1)
    w_all_ref[288:384, :] = eye.astype(F32).astype(BF16)
    turns = [wide_w if n == 0 else pltpu.roll(wide_w, LANES - 96 * n, 1) for n in range(3)]
    for n in range(3):
        piece = jnp.where(lane < FEATS, turns[n][0:96, 0:128], 0.0).astype(BF16)
        w_qkv_ref[:, n * 128 : n * 128 + 128] = piece
        if n:
            w_kv_ref[:, n * 128 - 128 : n * 128] = piece
    gq_ref[...] = jnp.zeros_like(gq_ref)
    gq_ref[:, 0:288] = jnp.broadcast_to(b_raw_ref[...], (128, 288))
    wide_b = gq_ref[...]
    b_col_ref[...] = wide_b.T
    for n in (1, 2):
        piece = jnp.where(lane[0:1] < FEATS, pltpu.roll(wide_b, LANES - 96 * n, 1)[0:1, 0:128], 0.0)
        b_kv_ref[:, n * 128 - 128 : n * 128] = k_feat_ref[:, n * 128 - 128 : n * 128] + piece
    gq_ref[...] = jnp.zeros_like(gq_ref)
    wide_table_ref[...] = jnp.zeros_like(wide_table_ref)
    wide_table_ref[0:HEADS, 0:TABLE] = table_ref[...]
    pl.semaphore_wait(barrier, nz - 1 + plane - 1)
    for a in range(2):
        for side in range(3):
            halo(a, side).start()
    load(0).wait()
    load(1).wait()

    def gather(t):
        wx, wy = window_at(t)
        for a in range(2):
            for ix in range(WIN):
                for iy in range(WIN):
                    n = ix * WIN + iy
                    tile = ext_ref[a, wx * WIN + SHIFT + ix, wy * WIN + SHIFT + iy].astype(F32)
                    win_ref[t, a, pl.ds(4 * n, 4), :] = tile[3:7]
                    send_f_ref[pl.ds(3 * n, 3), :] = tile[0:3]
            fwd_send_ref[t, a] = send_f_ref[...].astype(BF16)
        fwd(t).start()

    def first_gather(t, carry):
        gather(t)
        return carry

    lax.fori_loop(0, AHEAD, first_gather, 0)
    expand_table(wide_table_ref, ones_ref, bias_ref, wide_ref, flat_ref)

    def compute(t):
        wx, wy = window_at(t)
        last_x = (gx == nx - 1) & (wx == cells_x // WIN - 1)
        last_y = (gy == ny - 1) & (wy == cells_y // WIN - 1)
        last_z = gz == nz - 1
        fwd(t).wait_recv()
        for a in range(2):
            win_ref[t, a, OWN:ROWS, :] = fwd_recv_ref[t, a].astype(F32)[0 : ROWS - OWN]
        x = win_ref[t, 0]
        mean = jnp.mean(x, -1, keepdims=True)
        centered = x - mean
        rstd = lax.rsqrt(jnp.mean(centered * centered, -1, keepdims=True) + 1e-05)
        xhat = centered * rstd
        ln_ref[0:ROWS, :] = (xhat * gain_ref[...] + shift_ref[...]).astype(BF16)

        across = nt(w_all_ref[...], ln_ref[...])
        q_t = ((across[0:96] + b_col_ref[0:96, 0:1]) * (SCALE * LOG2E)).astype(BF16)
        k_t = (across[96:192] + b_col_ref[96:192, 0:1]).astype(BF16)
        v_t = (across[192:288] + b_col_ref[192:288, 0:1]).astype(BF16)
        ln_t = across[288:384].astype(BF16)
        marks = (
            q_feat_ref[0] * last_x.astype(F32)
            + q_feat_ref[1] * last_y.astype(F32)
            + q_feat_ref[2] * last_z.astype(F32)
        ).astype(BF16)
        for h in range(HEADS):
            q_ref[h * HDIM : (h + 1) * HDIM, h * LANES : (h + 1) * LANES] = q_t[h * HDIM : (h + 1) * HDIM]
            q_ref[96:112, h * LANES : (h + 1) * LANES] = marks
        kv = nn(ln_ref[0:ROWS, :], w_kv_ref[...]) + b_kv_ref[...]
        k = kv[:, 0:128].astype(BF16)
        v = kv[:, 128:256].astype(BF16)
        dyb_ref[0:ROWS, :] = win_ref[t, 1].astype(BF16)
        dy = dyb_ref[...]
        do_t = nt(w_proj_ref[...], dy)

        for h in range(HEADS):
            do_ref[h * HDIM : (h + 1) * HDIM, h * LANES : (h + 1) * LANES] = do_t[h * HDIM : (h + 1) * HDIM].astype(BF16)
        for u in range(0, HEADS * LANES, 256):
            at = pl.ds(u, min(256, HEADS * LANES - u))
            s = nn(k, q_ref[:, at]) + bias_ref[:, at]
            dp = nn(v, do_ref[:, at])
            e = jnp.exp2(s - jnp.max(s, 0, keepdims=True))
            e = e * (1.0 / jnp.sum(e, 0, keepdims=True))
            e_ref[0:ROWS, at] = e.astype(BF16)
            ds = e * (dp - jnp.sum(e * dp, 0, keepdims=True))
            acc_ref[:, at] += ds
            ds_ref[0:ROWS, at] = ds.astype(BF16)
        att = []
        for h in range(HEADS):
            at = pl.ds(h * LANES, LANES)
            att.append(nn(v_t[h * HDIM : (h + 1) * HDIM], e_ref[:, at]).astype(BF16))
            gq_ref[h * HDIM : (h + 1) * HDIM, :] = nn(k_t[h * HDIM : (h + 1) * HDIM], ds_ref[:, at]) * SCALE
        att = jnp.concatenate(att, 0)
        proj_ref[...] += nn(att, dy)
        grad_v = nt(e_ref[0:ROWS, :], do_ref[...])
        grad_k = nt(ds_ref[0:ROWS, :], q_ref[0:96, :]) * (1.0 / LOG2E)
        gq = gq_ref[...]
        wq_ref[0:96, 0:96] += nn(gq[0:96].astype(BF16), ln_ref[...])
        turned = gq.T[0:ROWS, 0:96]
        grad_q = turned.astype(BF16)
        grad_v = grad_v[:, 0:96]
        k_b = grad_k.astype(BF16)
        v_b = grad_v.astype(BF16)
        wkv_ref[:, 0:96] += nn(ln_t[:, 0:ROWS], k_b)
        wkv_ref[:, 128:224] += nn(ln_t[:, 0:ROWS], v_b)
        grad_in = (
            nt(grad_q, w_qkv_ref[:, 0:96])
            + nt(k_b, w_qkv_ref[:, 128:224])
            + nt(v_b, w_qkv_ref[:, 256:352])
        )
        for n, term in enumerate((turned, grad_k, grad_v, xhat * grad_in, grad_in)):
            rows_ref[n] += jnp.sum(term.reshape(ROWS // 8, 8, 96), 0)
        dhat = grad_in * gain_ref[...]
        first = jnp.mean(dhat, -1, keepdims=True)
        second = jnp.mean(dhat * xhat, -1, keepdims=True)
        dx_ref[t, 8 : 8 + ROWS, :] = win_ref[t, 1] + rstd * (dhat - first - xhat * second)
        ret_send_ref[t] = dx_ref[t, 8 + OWN : 8 + OWN + 160, :].astype(BF16)
        ret(t).start()

    sub = lax.broadcasted_iota(jnp.int32, (8, FEATS), 0)

    def merge(t):
        wx, wy = window_at(t)
        ret(t).wait_recv()
        back_f_ref[...] = ret_recv_ref[t].astype(F32)
        for ix in range(WIN):
            for iy in range(WIN):
                n = ix * WIN + iy
                low = back_f_ref[pl.ds(3 * n, 8), :]
                high = dx_ref[t, pl.ds(5 + 4 * n, 8), :]
                tile = jnp.where(sub < SHIFT, low, high).astype(BF16)
                out_ext_ref[wx * WIN + SHIFT + ix, wy * WIN + SHIFT + iy] = tile[0:7]

    def step(t, carry):
        @pl.when(t == 5 - AHEAD)
        def _():
            for a in range(2):
                for side in range(3):
                    halo(a, side).wait_recv()

        @pl.when(t + AHEAD < total)
        def _():
            gather(t + AHEAD)

        compute(t)

        @pl.when(t >= LAG)
        def _():
            merge(t - LAG)

        return carry

    lax.fori_loop(0, total, step, 0)

    block = plane * QUAD

    def put(row, value):
        while value.shape[0]:
            at = row % QUAD
            count = min(QUAD - at, value.shape[0])
            pay_ref[row // block, row % block // QUAD, at : at + count, 0 : value.shape[1]] = value[0:count]
            value = value[count:]
            row += count

    table_block = 384 // block
    put(0, wq_ref[...].T[0:96, 0:96])
    put(96, wkv_ref[:, 0:96])
    put(192, wkv_ref[:, 128:224])
    put(288, proj_ref[...])
    for k in range(1, nz):
        @pl.when(lax.rem(gz + k, nz) != table_block)
        def _():
            near(k).start()

    for side in range(3):
        edge(side).start()
    store_out(0).start()
    store_out(1).start()
    for n in range(5):
        put(438 + n, jnp.sum(rows_ref[n], 0, keepdims=True))
    fold_table(acc_ref, ones_ref, wide_ref, flat_ref, put)
    for k in range(1, nz):
        @pl.when(lax.rem(gz + k, nz) == table_block)
        def _():
            near(k).start()
    near_ref[gz] = pay_ref[gz]

    def last_merge(t, carry):
        merge(t)
        return carry

    lax.fori_loop(total - LAG, total, last_merge, 0)
    store_out(2).start()
    most_z = pl.ds(0, nz - 1)
    most_xy = pl.ds(0, plane - 1)
    wait_bytes(near_ref.at[most_z], near_recv)
    part_ref[...] = jnp.sum(near_ref[...], 0)
    for k in range(1, plane):
        far(k).start()
    far_ref[spot] = part_ref[spot]
    wait_bytes(far_ref.at[most_xy], far_recv)
    result_ref[gz, spot] = jnp.sum(far_ref[...], 0)
    for k in range(1, plane):
        share(k).start()
    wait_bytes(far_ref.at[most_xy], share_recv)
    for k in range(1, nz):
        final(k).start()
    for n in range(3):
        store_out(n).wait()
    for side in range(3):
        edge(side).wait()
    for a in range(2):
        for side in range(3):
            halo(a, side).wait_send()
    wait_bytes(fwd_send_ref, fwd_send)
    wait_bytes(ret_send_ref, ret_send)
    wait_bytes(near_ref.at[most_z], near_send)
    wait_bytes(far_ref.at[most_xy], far_send)
    wait_bytes(far_ref.at[most_xy], share_send)
    wait_bytes(near_ref.at[most_z], all_send)
    wait_bytes(near_ref.at[most_z], all_recv)


def whole_call(inputs, d_out, gain, shift, table, w_qkv, b_qkv, w_proj):
    cells_x, cells_y, cells_z, _ = inputs.shape
    count = (cells_x // WIN) * (cells_y // WIN)
    nz, plane = lax.axis_size("gz"), lax.axis_size("gx") * lax.axis_size("gy")
    ones = jnp.asarray(squeeze_ones(), BF16)
    consts = (gain[None, :], shift[None, :], table, ones, w_qkv, b_qkv[None, :])
    consts += (jnp.asarray(key_features()), jnp.asarray(query_features()), w_proj)
    outs = (
        jax.ShapeDtypeStruct(inputs.shape, BF16),
        jax.ShapeDtypeStruct((nz, plane, QUAD, 128), F32),
    )
    anywhere = pl.BlockSpec(memory_space=pl.ANY)
    inside = pl.BlockSpec(memory_space=pltpu.VMEM)
    dma = pltpu.SemaphoreType.DMA
    return pl.pallas_call(
        whole_kernel,
        in_specs=[anywhere] * 2 + [inside] * len(consts),
        out_specs=[anywhere, inside],
        out_shape=outs,
        scratch_shapes=[
            pltpu.VMEM((LANES, FEATS), BF16),
            pltpu.VMEM((96, 256), BF16),
            pltpu.VMEM((LANES, 128), F32),
            pltpu.VMEM((ROWS, 256), F32),
            pltpu.VMEM((96, LANES), BF16),
            pltpu.VMEM((8, SPREAD), F32),
            pltpu.VMEM((ROWS, HEADS * LANES), F32),
            pltpu.VMEM((ROWS, HEADS * LANES), F32),
            pltpu.VMEM((LANES, HEADS * LANES), BF16),
            pltpu.VMEM((LANES, HEADS * LANES), BF16),
            pltpu.VMEM((128, HEADS * LANES), BF16),
            pltpu.VMEM((128, HEADS * LANES), BF16),
            pltpu.VMEM((LANES, FEATS), BF16),
            pltpu.VMEM((128, LANES), F32),
            pltpu.VMEM((3, HEADS * 56, SPREAD), F32),
            pltpu.VMEM((HEADS * 56, SQUEEZED), F32),
            pltpu.VMEM((128, 128), F32),
            pltpu.VMEM((96, 256), F32),
            pltpu.VMEM((96, 96), F32),
            pltpu.VMEM((5, 8, 96), F32),
            pltpu.VMEM((2, cells_x + SHIFT, cells_y + SHIFT, cells_z, FEATS), BF16),
            pltpu.VMEM((count, 2, ROWS, FEATS), F32),
            pltpu.VMEM((160, FEATS), F32),
            pltpu.VMEM((LANES, FEATS), BF16),
            pltpu.VMEM((count, 368, FEATS), F32),
            pltpu.VMEM((160, FEATS), F32),
            pltpu.VMEM((cells_x + SHIFT, cells_y + SHIFT, cells_z, FEATS), BF16),
            pltpu.VMEM((count, 2, 160, FEATS), BF16),
            pltpu.VMEM((count, 2, 160, FEATS), BF16),
            pltpu.VMEM((count, 160, FEATS), BF16),
            pltpu.VMEM((count, 160, FEATS), BF16),
            pltpu.VMEM((nz, plane, QUAD, 128), F32),
            pltpu.VMEM((nz, plane, QUAD, 128), F32),
            pltpu.VMEM((plane, QUAD, 128), F32),
            pltpu.VMEM((plane, QUAD, 128), F32),
            dma((2,)),
            dma((2, 3)),
            dma((2, 3)),
            dma,
            dma((count,)),
            dma,
            dma((count,)),
            dma((3,)),
            dma((3,)),
            dma((3,)),
            dma,
            dma,
            dma,
            dma,
            dma,
            dma,
            dma,
            dma,
        ],
        compiler_params=pltpu.CompilerParams(
            vmem_limit_bytes=56 << 20, collective_id=0, has_side_effects=True
        ),
    )(inputs, d_out, *consts)


def shards(inputs, d_out, gain, shift, w_qkv, b_qkv, w_proj, rel_bias):
    field, sums = whole_call(inputs, d_out, gain, shift, rel_bias, w_qkv, b_qkv, w_proj)
    count = inputs.size // FEATS * lax.axis_size("gx") * lax.axis_size("gy") * lax.axis_size("gz")
    sums = sums.reshape(-1, 128) * float(count) ** -0.5
    weight = jnp.concatenate([sums[0:96, :96], sums[96:192, :96], sums[192:288, :96]], 1)
    proj = sums[288:384, :96]
    rel = sums[384:438].reshape(HEADS, SPREAD)[:, :TABLE]
    bias = sums[438:441, :96].reshape(-1)
    return field, weight, bias, proj, rel, sums[441, :96], sums[442, :96]


def solution(mesh):
    placed = (P("gx", "gy", "gz", None), P("gx", "gy", "gz", None), P(), P(), P(), P(), P(), P())
    return jax.shard_map(
        shards,
        mesh=mesh,
        in_specs=placed,
        out_specs=(P("gx", "gy", "gz", None), P(), P(), P(), P(), P(), P()),
        check_vma=False,
    )
```

```python
import functools

import jax
import jax.numpy as jnp
import numpy as np
from jax import lax
from jax.experimental import pallas as pl
from jax.experimental.pallas import tpu as pltpu
from jax.sharding import PartitionSpec as P

WIN = 7
SHIFT = 3
TOK = WIN**3
ROWS = 352
LANES = 384
FEATS = 96
HEADS = 3
HDIM = 32
PLANE = 49
WIDTH = 13
TABLE = WIDTH**3
SPREAD = 2304
SQUEEZED = 768
OWN = 196
OTHER = 147
AHEAD = 4
FIRST = 8
LAG = 3
QUAD = 4
MESH = pl.DeviceIdType.MESH
FAR = -(2.0**100)
NEVER = -1e30
LOG2E = 1.4426950408889634
SCALE = HDIM**-0.5
F32 = jnp.float32
BF16 = jnp.bfloat16


def nn(a, b):
    return lax.dot_general(a, b, (((1,), (0,)), ((), ())), preferred_element_type=F32)


def nt(a, b):
    return lax.dot_general(a, b, (((1,), (1,)), ((), ())), preferred_element_type=F32)


def token_place(count):
    p = np.arange(count)
    n = np.where(p < OWN, p // 4, (p - OWN) // 3)
    z = np.where(p < OWN, p % 4, 4 + (p - OWN) % 3)
    return n // 7, n % 7, z


def token_late(count):
    return np.stack([(place >= WIN - SHIFT).astype(np.float32) for place in token_place(count)])


def squeeze_ones():
    lane = np.arange(SQUEEZED)
    m = lane - LANES
    own = lane // 28 * 169 + lane % 28 // 4 * 13 + lane % 4
    other = m // 21 * 169 + m % 21 // 3 * 13 + 4 + m % 3
    place = np.where(lane < 364, own, np.where((m >= 0) & (m < 273), other, -1))
    return (np.arange(SPREAD)[:, None] == place[None, :]).astype(np.float32)


def key_features():
    late = token_late(ROWS)
    out = np.zeros((ROWS, 256), np.float32)
    for d in range(3):
        out[:, 96 + 2 * d] = late[d]
        out[:, 97 + 2 * d] = 1 - late[d]
    return out


def query_features():
    late = token_late(LANES)
    out = np.zeros((3, 16, LANES), np.float32)
    for d in range(3):
        out[d, 2 * d] = FAR * (1 - late[d])
        out[d, 2 * d + 1] = FAR * late[d]
    return out


def pieces(x, count):
    out = []
    for _ in range(count):
        piece = x.astype(BF16)
        out.append(piece)
        x = x - piece.astype(F32)
    return out


def expand_table(table_ref, ones_ref, bias_ref, wide_ref, flat_ref):
    for h in range(HEADS):
        row = jnp.broadcast_to(table_ref[h : h + 1, :] * LOG2E, (8, SPREAD))
        row = pltpu.roll(row, 0, 1, stride=1, stride_axis=0)
        for jy in range(WIN):
            moved = pltpu.roll(row, SPREAD - 13 * (6 - jy) - 6, 1)
            for n, piece in enumerate(pieces(moved, 3)):
                wide_ref[n, h * 56 + jy * 8 : h * 56 + jy * 8 + 8, :] = piece.astype(F32)
    total = None
    for n in range(3):
        part = nn(wide_ref[n].astype(BF16), ones_ref[...])
        total = part if total is None else total + part
    flat_ref[...] = total
    lane = lax.broadcasted_iota(jnp.int32, (56, LANES), 1)
    for h in range(HEADS):
        for jx in range(WIN):
            own = pltpu.roll(flat_ref[h * 56 : h * 56 + 56, 0:LANES], (LANES - 28 * (6 - jx)) % LANES, 1)
            other = pltpu.roll(
                flat_ref[h * 56 : h * 56 + 56, LANES:SQUEEZED], (LANES + OWN - 21 * (6 - jx)) % LANES, 1
            )
            both = jnp.where(lane < OWN, own, jnp.where(lane < TOK, other, 0.0))
            for jy in range(WIN):
                n = jx * 7 + jy
                bias_ref[pl.ds(4 * n, 4), h * LANES : (h + 1) * LANES] = both[jy * 8 : jy * 8 + 4]
                bias_ref[pl.ds(OWN + 3 * n, 3), h * LANES : (h + 1) * LANES] = both[jy * 8 + 4 : jy * 8 + 7]
        bias_ref[TOK:ROWS, h * LANES : (h + 1) * LANES] = jnp.full((ROWS - TOK, LANES), NEVER, F32)


def fold_table(sums_ref, ones_ref, wide_ref, flat_ref, put):
    sub = lax.broadcasted_iota(jnp.int32, (8, LANES), 0)
    lane = lax.broadcasted_iota(jnp.int32, (8, LANES), 1)
    for h in range(HEADS):
        for jy in range(WIN):
            own = jnp.zeros((8, LANES), F32)
            other = jnp.zeros((8, LANES), F32)
            for jx in range(WIN):
                n = jx * 7 + jy
                low = sums_ref[pl.ds(4 * n, 8), h * LANES : (h + 1) * LANES]
                high = sums_ref[pl.ds(OWN + 3 * n - 4, 8), h * LANES : (h + 1) * LANES]
                block = jnp.where(sub < 4, low, high)
                own = own + pltpu.roll(jnp.where(lane < OWN, block, 0.0), 28 * (6 - jx), 1)
                rest = jnp.where((lane >= OWN) & (lane < TOK), block, 0.0)
                other = other + pltpu.roll(rest, (LANES - OWN + 21 * (6 - jx)) % LANES, 1)
            at = h * 56 + jy * 8
            flat_ref[at : at + 8, 0:LANES] = jnp.where(sub < WIN, own, 0.0)
            flat_ref[at : at + 8, LANES:SQUEEZED] = jnp.where(sub < WIN, other, 0.0)
    spread = None
    for piece in pieces(flat_ref[...], 3):
        part = nt(piece, ones_ref[...])
        spread = part if spread is None else spread + part
    wide_ref[0] = spread
    for h in range(HEADS):
        total = jnp.zeros((8, SPREAD), F32)
        for jy in range(WIN):
            block = wide_ref[0, h * 56 + jy * 8 : h * 56 + jy * 8 + 8, :]
            total = total + pltpu.roll(block, 13 * (6 - jy), 1)
        line = jnp.zeros((1, SPREAD), F32)
        for jz in range(WIN):
            line = line + pltpu.roll(total, 6 - jz, 1)[jz : jz + 1]
        for c in range(SPREAD // 128):
            put(384 + h * 18 + c, line[:, c * 128 : c * 128 + 128])


def window_at(t):
    inner = jnp.where(t < FIRST, t, t - 7)
    edge = t - FIRST
    side_x = jnp.where(edge < 4, 3, edge - 4)
    side_y = jnp.where(edge < 4, edge, 3)
    is_edge = (t >= FIRST) & (t < FIRST + 7)
    return jnp.where(is_edge, side_x, inner // 3), jnp.where(is_edge, side_y, inner % 3)


def whole_kernel(
    x_hbm,
    dy_hbm,
    gain_ref,
    shift_ref,
    table_ref,
    ones_ref,
    w_raw_ref,
    b_raw_ref,
    k_feat_ref,
    q_feat_ref,
    w_proj_ref,
    out_hbm,
    result_ref,
    w_all_ref,
    w_kv_ref,
    b_col_ref,
    b_kv_ref,
    w_qkv_ref,
    wide_table_ref,
    bias_ref,
    acc_ref,
    e_ref,
    ds_ref,
    q_ref,
    do_ref,
    ln_ref,
    gq_ref,
    wide_ref,
    flat_ref,
    wq_ref,
    wkv_ref,
    proj_ref,
    rows_ref,
    ext_ref,
    win_ref,
    send_f_ref,
    dyb_ref,
    dx_ref,
    back_f_ref,
    out_ext_ref,
    fwd_send_ref,
    fwd_recv_ref,
    ret_send_ref,
    ret_recv_ref,
    pay_ref,
    near_ref,
    part_ref,
    far_ref,
    load_sem,
    halo_send,
    halo_recv,
    fwd_send,
    fwd_recv,
    ret_send,
    ret_recv,
    out_sem,
    edge_send,
    edge_recv,
    near_send,
    near_recv,
    far_send,
    far_recv,
    share_send,
    share_recv,
    all_send,
    all_recv,
):
    nx, ny, nz = lax.axis_size("gx"), lax.axis_size("gy"), lax.axis_size("gz")
    gx, gy, gz = lax.axis_index("gx"), lax.axis_index("gy"), lax.axis_index("gz")
    plane = nx * ny
    spot = gx * ny + gy
    cells_x, cells_y = x_hbm.shape[0], x_hbm.shape[1]
    total = (cells_x // WIN) * (cells_y // WIN)

    def peer_z(k):
        return {"gz": lax.rem(gz + k, nz)}

    def peer_xy(k):
        other = lax.rem(spot + k, plane)
        return {"gx": other // ny, "gy": lax.rem(other, ny)}

    barrier = pltpu.get_barrier_semaphore()
    for k in range(1, nz):
        pl.semaphore_signal(barrier, inc=1, device_id=peer_z(k), device_id_type=MESH)
    for k in range(1, plane):
        pl.semaphore_signal(barrier, inc=1, device_id=peer_xy(k), device_id_type=MESH)

    def load(a):
        source = (x_hbm, dy_hbm)[a]
        return pltpu.make_async_copy(
            source, ext_ref.at[a, pl.ds(0, cells_x), pl.ds(0, cells_y)], load_sem.at[a]
        )

    def halo(a, side):
        source = (x_hbm, dy_hbm)[a]
        px, py = ((1, 0), (0, 1), (1, 1))[side]
        from_x = pl.ds(0, SHIFT) if px else pl.ds(0, cells_x)
        from_y = pl.ds(0, SHIFT) if py else pl.ds(0, cells_y)
        to_x = pl.ds(cells_x, SHIFT) if px else pl.ds(0, cells_x)
        to_y = pl.ds(cells_y, SHIFT) if py else pl.ds(0, cells_y)
        return pltpu.make_async_remote_copy(
            src_ref=source.at[from_x, from_y],
            dst_ref=ext_ref.at[a, to_x, to_y],
            send_sem=halo_send.at[a, side],
            recv_sem=halo_recv.at[a, side],
            device_id={"gx": lax.rem(gx + nx - px, nx), "gy": lax.rem(gy + ny - py, ny)},
            device_id_type=MESH,
        )

    def fwd(t):
        return pltpu.make_async_remote_copy(
            src_ref=fwd_send_ref.at[t],
            dst_ref=fwd_recv_ref.at[t],
            send_sem=fwd_send,
            recv_sem=fwd_recv.at[t],
            device_id=peer_z(nz - 1),
            device_id_type=MESH,
        )

    def ret(t):
        return pltpu.make_async_remote_copy(
            src_ref=ret_send_ref.at[t],
            dst_ref=ret_recv_ref.at[t],
            send_sem=ret_send,
            recv_sem=ret_recv.at[t],
            device_id=peer_z(1),
            device_id_type=MESH,
        )

    def edge(side):
        px, py = ((1, 0), (0, 1), (1, 1))[side]
        from_x = pl.ds(cells_x, SHIFT) if px else pl.ds(SHIFT, cells_x - SHIFT)
        from_y = pl.ds(cells_y, SHIFT) if py else pl.ds(SHIFT, cells_y - SHIFT)
        to_x = pl.ds(0, SHIFT) if px else pl.ds(SHIFT, cells_x - SHIFT)
        to_y = pl.ds(0, SHIFT) if py else pl.ds(SHIFT, cells_y - SHIFT)
        return pltpu.make_async_remote_copy(
            src_ref=out_ext_ref.at[from_x, from_y],
            dst_ref=out_hbm.at[to_x, to_y],
            send_sem=edge_send.at[side],
            recv_sem=edge_recv.at[side],
            device_id={"gx": lax.rem(gx + px, nx), "gy": lax.rem(gy + py, ny)},
            device_id_type=MESH,
        )

    def store_out(n):
        first, last = ((SHIFT, 10), (24, cells_x), (10, 24))[n]
        rows = pl.ds(first, last - first)
        inner_y = pl.ds(SHIFT, cells_y - SHIFT)
        return pltpu.make_async_copy(out_ext_ref.at[rows, inner_y], out_hbm.at[rows, inner_y], out_sem.at[n])

    def wait_bytes(like, sem):
        pltpu.make_async_copy(like, like, sem).wait()

    def near(k):
        return pltpu.make_async_remote_copy(
            src_ref=pay_ref.at[lax.rem(gz + k, nz)],
            dst_ref=near_ref.at[gz],
            send_sem=near_send,
            recv_sem=near_recv,
            device_id=peer_z(k),
            device_id_type=MESH,
        )

    def far(k):
        return pltpu.make_async_remote_copy(
            src_ref=part_ref.at[lax.rem(spot + k, plane)],
            dst_ref=far_ref.at[spot],
            send_sem=far_send,
            recv_sem=far_recv,
            device_id=peer_xy(k),
            device_id_type=MESH,
        )

    def share(k):
        return pltpu.make_async_remote_copy(
            src_ref=result_ref.at[gz, spot],
            dst_ref=result_ref.at[gz, spot],
            send_sem=share_send,
            recv_sem=share_recv,
            device_id=peer_xy(k),
            device_id_type=MESH,
        )

    def final(k):
        return pltpu.make_async_remote_copy(
            src_ref=result_ref.at[gz],
            dst_ref=result_ref.at[gz],
            send_sem=all_send,
            recv_sem=all_recv,
            device_id=peer_z(k),
            device_id_type=MESH,
        )

    load(0).start()
    load(1).start()
    acc_ref[...] = jnp.zeros_like(acc_ref)
    e_ref[...] = jnp.zeros_like(e_ref)
    ds_ref[...] = jnp.zeros_like(ds_ref)
    q_ref[...] = jnp.zeros_like(q_ref)
    do_ref[...] = jnp.zeros_like(do_ref)
    wq_ref[...] = jnp.zeros_like(wq_ref)
    wkv_ref[...] = jnp.zeros_like(wkv_ref)
    proj_ref[...] = jnp.zeros_like(proj_ref)
    rows_ref[...] = jnp.zeros_like(rows_ref)
    gq_ref[...] = jnp.zeros_like(gq_ref)
    ln_ref[...] = jnp.zeros_like(ln_ref)
    dyb_ref[...] = jnp.zeros_like(dyb_ref)
    send_f_ref[...] = jnp.zeros_like(send_f_ref)
    pay_ref[...] = jnp.zeros_like(pay_ref)
    for t in range(total):
        dx_ref[t, 0:8, :] = jnp.zeros((8, FEATS), F32)
        dx_ref[t, 360:368, :] = jnp.zeros((8, FEATS), F32)
    gq_ref[0:96, 0:288] = w_raw_ref[...].astype(F32)
    wide_w = gq_ref[...]
    lane = lax.broadcasted_iota(jnp.int32, (96, 128), 1)
    w_all_ref[0:288, :] = wide_w.T[0:288, 0:96].astype(BF16)
    eye = lax.broadcasted_iota(jnp.int32, (96, 96), 0) == lax.broadcasted_iota(jnp.int32, (96, 96), 1)
    w_all_ref[288:384, :] = eye.astype(F32).astype(BF16)
    turns = [wide_w if n == 0 else pltpu.roll(wide_w, LANES - 96 * n, 1) for n in range(3)]
    for n in range(3):
        piece = jnp.where(lane < FEATS, turns[n][0:96, 0:128], 0.0).astype(BF16)
        w_qkv_ref[:, n * 128 : n * 128 + 128] = piece
        if n:
            w_kv_ref[:, n * 128 - 128 : n * 128] = piece
    gq_ref[...] = jnp.zeros_like(gq_ref)
    gq_ref[:, 0:288] = jnp.broadcast_to(b_raw_ref[...], (128, 288))
    wide_b = gq_ref[...]
    b_col_ref[...] = wide_b.T
    for n in (1, 2):
        piece = jnp.where(lane[0:1] < FEATS, pltpu.roll(wide_b, LANES - 96 * n, 1)[0:1, 0:128], 0.0)
        b_kv_ref[:, n * 128 - 128 : n * 128] = k_feat_ref[:, n * 128 - 128 : n * 128] + piece
    gq_ref[...] = jnp.zeros_like(gq_ref)
    wide_table_ref[...] = jnp.zeros_like(wide_table_ref)
    wide_table_ref[0:HEADS, 0:TABLE] = table_ref[...]
    pl.semaphore_wait(barrier, nz - 1 + plane - 1)
    for a in range(2):
        for side in range(3):
            halo(a, side).start()
    load(0).wait()
    load(1).wait()

    def gather(t):
        wx, wy = window_at(t)
        for a in range(2):
            for ix in range(WIN):
                for iy in range(WIN):
                    n = ix * WIN + iy
                    tile = ext_ref[a, wx * WIN + SHIFT + ix, wy * WIN + SHIFT + iy].astype(F32)
                    win_ref[t, a, pl.ds(4 * n, 4), :] = tile[3:7]
                    send_f_ref[pl.ds(3 * n, 3), :] = tile[0:3]
            fwd_send_ref[t, a] = send_f_ref[...].astype(BF16)
        fwd(t).start()

    def first_gather(t, carry):
        gather(t)
        return carry

    lax.fori_loop(0, AHEAD, first_gather, 0)
    expand_table(wide_table_ref, ones_ref, bias_ref, wide_ref, flat_ref)

    def compute(t):
        wx, wy = window_at(t)
        last_x = (gx == nx - 1) & (wx == cells_x // WIN - 1)
        last_y = (gy == ny - 1) & (wy == cells_y // WIN - 1)
        last_z = gz == nz - 1
        fwd(t).wait_recv()
        for a in range(2):
            win_ref[t, a, OWN:ROWS, :] = fwd_recv_ref[t, a].astype(F32)[0 : ROWS - OWN]
        x = win_ref[t, 0]
        mean = jnp.mean(x, -1, keepdims=True)
        centered = x - mean
        rstd = lax.rsqrt(jnp.mean(centered * centered, -1, keepdims=True) + 1e-05)
        xhat = centered * rstd
        ln_ref[0:ROWS, :] = (xhat * gain_ref[...] + shift_ref[...]).astype(BF16)

        across = nt(w_all_ref[...], ln_ref[...])
        q_t = ((across[0:96] + b_col_ref[0:96, 0:1]) * (SCALE * LOG2E)).astype(BF16)
        k_t = (across[96:192] + b_col_ref[96:192, 0:1]).astype(BF16)
        v_t = (across[192:288] + b_col_ref[192:288, 0:1]).astype(BF16)
        ln_t = across[288:384].astype(BF16)
        marks = (
            q_feat_ref[0] * last_x.astype(F32)
            + q_feat_ref[1] * last_y.astype(F32)
            + q_feat_ref[2] * last_z.astype(F32)
        ).astype(BF16)
        for h in range(HEADS):
            q_ref[h * HDIM : (h + 1) * HDIM, h * LANES : (h + 1) * LANES] = q_t[h * HDIM : (h + 1) * HDIM]
            q_ref[96:112, h * LANES : (h + 1) * LANES] = marks
        kv = nn(ln_ref[0:ROWS, :], w_kv_ref[...]) + b_kv_ref[...]
        k = kv[:, 0:128].astype(BF16)
        v = kv[:, 128:256].astype(BF16)
        dyb_ref[0:ROWS, :] = win_ref[t, 1].astype(BF16)
        dy = dyb_ref[...]
        do_t = nt(w_proj_ref[...], dy)

        for h in range(HEADS):
            do_ref[h * HDIM : (h + 1) * HDIM, h * LANES : (h + 1) * LANES] = do_t[h * HDIM : (h + 1) * HDIM].astype(BF16)
        for u in range(0, HEADS * LANES, 256):
            at = pl.ds(u, min(256, HEADS * LANES - u))
            s = nn(k, q_ref[:, at]) + bias_ref[:, at]
            dp = nn(v, do_ref[:, at])
            e = jnp.exp2(s - jnp.max(s, 0, keepdims=True))
            e = e * (1.0 / jnp.sum(e, 0, keepdims=True))
            e_ref[0:ROWS, at] = e.astype(BF16)
            ds = e * (dp - jnp.sum(e * dp, 0, keepdims=True))
            acc_ref[:, at] += ds
            ds_ref[0:ROWS, at] = ds.astype(BF16)
        att = []
        for h in range(HEADS):
            at = pl.ds(h * LANES, LANES)
            att.append(nn(v_t[h * HDIM : (h + 1) * HDIM], e_ref[:, at]).astype(BF16))
            gq_ref[h * HDIM : (h + 1) * HDIM, :] = nn(k_t[h * HDIM : (h + 1) * HDIM], ds_ref[:, at]) * SCALE
        att = jnp.concatenate(att, 0)
        proj_ref[...] += nn(att, dy)
        grad_v = nt(e_ref[0:ROWS, :], do_ref[...])
        grad_k = nt(ds_ref[0:ROWS, :], q_ref[0:96, :]) * (1.0 / LOG2E)
        gq = gq_ref[...]
        wq_ref[0:96, 0:96] += nn(gq[0:96].astype(BF16), ln_ref[...])
        turned = gq.T[0:ROWS, 0:96]
        grad_q = turned.astype(BF16)
        grad_v = grad_v[:, 0:96]
        k_b = grad_k.astype(BF16)
        v_b = grad_v.astype(BF16)
        wkv_ref[:, 0:96] += nn(ln_t[:, 0:ROWS], k_b)
        wkv_ref[:, 128:224] += nn(ln_t[:, 0:ROWS], v_b)
        grad_in = (
            nt(grad_q, w_qkv_ref[:, 0:96])
            + nt(k_b, w_qkv_ref[:, 128:224])
            + nt(v_b, w_qkv_ref[:, 256:352])
        )
        for n, term in enumerate((turned, grad_k, grad_v, xhat * grad_in, grad_in)):
            rows_ref[n] += jnp.sum(term.reshape(ROWS // 8, 8, 96), 0)
        dhat = grad_in * gain_ref[...]
        first = jnp.mean(dhat, -1, keepdims=True)
        second = jnp.mean(dhat * xhat, -1, keepdims=True)
        dx_ref[t, 8 : 8 + ROWS, :] = win_ref[t, 1] + rstd * (dhat - first - xhat * second)
        ret_send_ref[t] = dx_ref[t, 8 + OWN : 8 + OWN + 160, :].astype(BF16)
        ret(t).start()

    sub = lax.broadcasted_iota(jnp.int32, (8, FEATS), 0)

    def merge(t):
        wx, wy = window_at(t)
        ret(t).wait_recv()
        back_f_ref[...] = ret_recv_ref[t].astype(F32)
        for ix in range(WIN):
            for iy in range(WIN):
                n = ix * WIN + iy
                low = back_f_ref[pl.ds(3 * n, 8), :]
                high = dx_ref[t, pl.ds(5 + 4 * n, 8), :]
                tile = jnp.where(sub < SHIFT, low, high).astype(BF16)
                out_ext_ref[wx * WIN + SHIFT + ix, wy * WIN + SHIFT + iy] = tile[0:7]

    def step(t, carry):
        @pl.when(t == FIRST - AHEAD)
        def _():
            for a in range(2):
                for side in range(3):
                    halo(a, side).wait_recv()

        @pl.when(t + AHEAD < total)
        def _():
            gather(t + AHEAD)

        compute(t)

        @pl.when(t >= LAG)
        def _():
            merge(t - LAG)

        return carry

    lax.fori_loop(0, total, step, 0)

    block = plane * QUAD

    def put(row, value):
        while value.shape[0]:
            at = row % QUAD
            count = min(QUAD - at, value.shape[0])
            pay_ref[row // block, row % block // QUAD, at : at + count, 0 : value.shape[1]] = value[0:count]
            value = value[count:]
            row += count

    table_block = 384 // block
    put(0, wq_ref[...].T[0:96, 0:96])
    put(96, wkv_ref[:, 0:96])
    put(192, wkv_ref[:, 128:224])
    put(288, proj_ref[...])
    for k in range(1, nz):
        @pl.when(lax.rem(gz + k, nz) != table_block)
        def _():
            near(k).start()

    edge(0).start()
    edge(2).start()
    store_out(0).start()
    store_out(1).start()
    for n in range(5):
        put(438 + n, jnp.sum(rows_ref[n], 0, keepdims=True))
    fold_table(acc_ref, ones_ref, wide_ref, flat_ref, put)
    for k in range(1, nz):
        @pl.when(lax.rem(gz + k, nz) == table_block)
        def _():
            near(k).start()
    near_ref[gz] = pay_ref[gz]

    def last_merge(t, carry):
        merge(t)
        return carry

    lax.fori_loop(total - LAG, total, last_merge, 0)
    edge(1).start()
    store_out(2).start()
    most_z = pl.ds(0, nz - 1)
    most_xy = pl.ds(0, plane - 1)
    wait_bytes(near_ref.at[most_z], near_recv)
    part_ref[...] = jnp.sum(near_ref[...], 0)
    for k in range(1, plane):
        far(k).start()
    far_ref[spot] = part_ref[spot]
    wait_bytes(far_ref.at[most_xy], far_recv)
    result_ref[gz, spot] = jnp.sum(far_ref[...], 0)
    for k in range(1, plane):
        share(k).start()
    wait_bytes(far_ref.at[most_xy], share_recv)
    for k in range(1, nz):
        final(k).start()
    for n in range(3):
        store_out(n).wait()
    for side in range(3):
        edge(side).wait()
    for a in range(2):
        for side in range(3):
            halo(a, side).wait_send()
    wait_bytes(fwd_send_ref, fwd_send)
    wait_bytes(ret_send_ref, ret_send)
    wait_bytes(near_ref.at[most_z], near_send)
    wait_bytes(far_ref.at[most_xy], far_send)
    wait_bytes(far_ref.at[most_xy], share_send)
    wait_bytes(near_ref.at[most_z], all_send)
    wait_bytes(near_ref.at[most_z], all_recv)


def whole_call(inputs, d_out, gain, shift, table, w_qkv, b_qkv, w_proj):
    cells_x, cells_y, cells_z, _ = inputs.shape
    count = (cells_x // WIN) * (cells_y // WIN)
    nz, plane = lax.axis_size("gz"), lax.axis_size("gx") * lax.axis_size("gy")
    ones = jnp.asarray(squeeze_ones(), BF16)
    consts = (gain[None, :], shift[None, :], table, ones, w_qkv, b_qkv[None, :])
    consts += (jnp.asarray(key_features()), jnp.asarray(query_features()), w_proj)
    outs = (
        jax.ShapeDtypeStruct(inputs.shape, BF16),
        jax.ShapeDtypeStruct((nz, plane, QUAD, 128), F32),
    )
    anywhere = pl.BlockSpec(memory_space=pl.ANY)
    inside = pl.BlockSpec(memory_space=pltpu.VMEM)
    dma = pltpu.SemaphoreType.DMA
    return pl.pallas_call(
        whole_kernel,
        in_specs=[anywhere] * 2 + [inside] * len(consts),
        out_specs=[anywhere, inside],
        out_shape=outs,
        scratch_shapes=[
            pltpu.VMEM((LANES, FEATS), BF16),
            pltpu.VMEM((96, 256), BF16),
            pltpu.VMEM((LANES, 128), F32),
            pltpu.VMEM((ROWS, 256), F32),
            pltpu.VMEM((96, LANES), BF16),
            pltpu.VMEM((8, SPREAD), F32),
            pltpu.VMEM((ROWS, HEADS * LANES), F32),
            pltpu.VMEM((ROWS, HEADS * LANES), F32),
            pltpu.VMEM((LANES, HEADS * LANES), BF16),
            pltpu.VMEM((LANES, HEADS * LANES), BF16),
            pltpu.VMEM((128, HEADS * LANES), BF16),
            pltpu.VMEM((128, HEADS * LANES), BF16),
            pltpu.VMEM((LANES, FEATS), BF16),
            pltpu.VMEM((128, LANES), F32),
            pltpu.VMEM((3, HEADS * 56, SPREAD), F32),
            pltpu.VMEM((HEADS * 56, SQUEEZED), F32),
            pltpu.VMEM((128, 128), F32),
            pltpu.VMEM((96, 256), F32),
            pltpu.VMEM((96, 96), F32),
            pltpu.VMEM((5, 8, 96), F32),
            pltpu.VMEM((2, cells_x + SHIFT, cells_y + SHIFT, cells_z, FEATS), BF16),
            pltpu.VMEM((count, 2, ROWS, FEATS), F32),
            pltpu.VMEM((160, FEATS), F32),
            pltpu.VMEM((LANES, FEATS), BF16),
            pltpu.VMEM((count, 368, FEATS), F32),
            pltpu.VMEM((160, FEATS), F32),
            pltpu.VMEM((cells_x + SHIFT, cells_y + SHIFT, cells_z, FEATS), BF16),
            pltpu.VMEM((count, 2, 160, FEATS), BF16),
            pltpu.VMEM((count, 2, 160, FEATS), BF16),
            pltpu.VMEM((count, 160, FEATS), BF16),
            pltpu.VMEM((count, 160, FEATS), BF16),
            pltpu.VMEM((nz, plane, QUAD, 128), F32),
            pltpu.VMEM((nz, plane, QUAD, 128), F32),
            pltpu.VMEM((plane, QUAD, 128), F32),
            pltpu.VMEM((plane, QUAD, 128), F32),
            dma((2,)),
            dma((2, 3)),
            dma((2, 3)),
            dma,
            dma((count,)),
            dma,
            dma((count,)),
            dma((3,)),
            dma((3,)),
            dma((3,)),
            dma,
            dma,
            dma,
            dma,
            dma,
            dma,
            dma,
            dma,
        ],
        compiler_params=pltpu.CompilerParams(
            vmem_limit_bytes=56 << 20, collective_id=0, has_side_effects=True
        ),
    )(inputs, d_out, *consts)


def shards(inputs, d_out, gain, shift, w_qkv, b_qkv, w_proj, rel_bias):
    field, sums = whole_call(inputs, d_out, gain, shift, rel_bias, w_qkv, b_qkv, w_proj)
    count = inputs.size // FEATS * lax.axis_size("gx") * lax.axis_size("gy") * lax.axis_size("gz")
    sums = sums.reshape(-1, 128) * float(count) ** -0.5
    weight = jnp.concatenate([sums[0:96, :96], sums[96:192, :96], sums[192:288, :96]], 1)
    proj = sums[288:384, :96]
    rel = sums[384:438].reshape(HEADS, SPREAD)[:, :TABLE]
    bias = sums[438:441, :96].reshape(-1)
    return field, weight, bias, proj, rel, sums[441, :96], sums[442, :96]


def solution(mesh):
    placed = (P("gx", "gy", "gz", None), P("gx", "gy", "gz", None), P(), P(), P(), P(), P(), P())
    return jax.shard_map(
        shards,
        mesh=mesh,
        in_specs=placed,
        out_specs=(P("gx", "gy", "gz", None), P(), P(), P(), P(), P(), P()),
        check_vma=False,
    )
```

```python
import functools

import jax
import jax.numpy as jnp
import numpy as np
from jax import lax
from jax.experimental import pallas as pl
from jax.experimental.pallas import tpu as pltpu
from jax.sharding import PartitionSpec as P

WIN = 7
SHIFT = 3
TOK = WIN**3
ROWS = 352
LANES = 384
FEATS = 96
HEADS = 3
HDIM = 32
PLANE = 49
WIDTH = 13
TABLE = WIDTH**3
SPREAD = 2304
SQUEEZED = 768
OWN = 196
OTHER = 147
AHEAD = 4
LAG = 3
QUAD = 4
MESH = pl.DeviceIdType.MESH
FAR = -(2.0**100)
NEVER = -1e30
LOG2E = 1.4426950408889634
SCALE = HDIM**-0.5
F32 = jnp.float32
BF16 = jnp.bfloat16


def nn(a, b):
    return lax.dot_general(a, b, (((1,), (0,)), ((), ())), preferred_element_type=F32)


def nt(a, b):
    return lax.dot_general(a, b, (((1,), (1,)), ((), ())), preferred_element_type=F32)


def token_place(count):
    p = np.arange(count)
    n = np.where(p < OWN, p // 4, (p - OWN) // 3)
    z = np.where(p < OWN, p % 4, 4 + (p - OWN) % 3)
    return n // 7, n % 7, z


def token_late(count):
    return np.stack([(place >= WIN - SHIFT).astype(np.float32) for place in token_place(count)])


def squeeze_ones():
    lane = np.arange(SQUEEZED)
    m = lane - LANES
    own = lane // 28 * 169 + lane % 28 // 4 * 13 + lane % 4
    other = m // 21 * 169 + m % 21 // 3 * 13 + 4 + m % 3
    place = np.where(lane < 364, own, np.where((m >= 0) & (m < 273), other, -1))
    return (np.arange(SPREAD)[:, None] == place[None, :]).astype(np.float32)


def key_features():
    late = token_late(ROWS)
    out = np.zeros((ROWS, 256), np.float32)
    for d in range(3):
        out[:, 96 + 2 * d] = late[d]
        out[:, 97 + 2 * d] = 1 - late[d]
    return out


def query_features():
    late = token_late(LANES)
    out = np.zeros((3, 16, LANES), np.float32)
    for d in range(3):
        out[d, 2 * d] = FAR * (1 - late[d])
        out[d, 2 * d + 1] = FAR * late[d]
    return out


def pieces(x, count):
    out = []
    for _ in range(count):
        piece = x.astype(BF16)
        out.append(piece)
        x = x - piece.astype(F32)
    return out


def expand_table(table_ref, ones_ref, bias_ref, wide_ref, flat_ref):
    for h in range(HEADS):
        row = jnp.broadcast_to(table_ref[h : h + 1, :] * LOG2E, (8, SPREAD))
        row = pltpu.roll(row, 0, 1, stride=1, stride_axis=0)
        for jy in range(WIN):
            moved = pltpu.roll(row, SPREAD - 13 * (6 - jy) - 6, 1)
            for n, piece in enumerate(pieces(moved, 3)):
                wide_ref[n, h * 56 + jy * 8 : h * 56 + jy * 8 + 8, :] = piece.astype(F32)
    total = None
    for n in range(3):
        part = nn(wide_ref[n].astype(BF16), ones_ref[...])
        total = part if total is None else total + part
    flat_ref[...] = total
    lane = lax.broadcasted_iota(jnp.int32, (56, LANES), 1)
    for h in range(HEADS):
        for jx in range(WIN):
            own = pltpu.roll(flat_ref[h * 56 : h * 56 + 56, 0:LANES], (LANES - 28 * (6 - jx)) % LANES, 1)
            other = pltpu.roll(
                flat_ref[h * 56 : h * 56 + 56, LANES:SQUEEZED], (LANES + OWN - 21 * (6 - jx)) % LANES, 1
            )
            both = jnp.where(lane < OWN, own, jnp.where(lane < TOK, other, 0.0))
            for jy in range(WIN):
                n = jx * 7 + jy
                bias_ref[pl.ds(4 * n, 4), h * LANES : (h + 1) * LANES] = both[jy * 8 : jy * 8 + 4]
                bias_ref[pl.ds(OWN + 3 * n, 3), h * LANES : (h + 1) * LANES] = both[jy * 8 + 4 : jy * 8 + 7]
        bias_ref[TOK:ROWS, h * LANES : (h + 1) * LANES] = jnp.full((ROWS - TOK, LANES), NEVER, F32)


def fold_table(sums_ref, ones_ref, wide_ref, flat_ref, put):
    sub = lax.broadcasted_iota(jnp.int32, (8, LANES), 0)
    lane = lax.broadcasted_iota(jnp.int32, (8, LANES), 1)
    for h in range(HEADS):
        for jy in range(WIN):
            own = jnp.zeros((8, LANES), F32)
            other = jnp.zeros((8, LANES), F32)
            for jx in range(WIN):
                n = jx * 7 + jy
                low = sums_ref[pl.ds(4 * n, 8), h * LANES : (h + 1) * LANES]
                high = sums_ref[pl.ds(OWN + 3 * n - 4, 8), h * LANES : (h + 1) * LANES]
                block = jnp.where(sub < 4, low, high)
                own = own + pltpu.roll(jnp.where(lane < OWN, block, 0.0), 28 * (6 - jx), 1)
                rest = jnp.where((lane >= OWN) & (lane < TOK), block, 0.0)
                other = other + pltpu.roll(rest, (LANES - OWN + 21 * (6 - jx)) % LANES, 1)
            at = h * 56 + jy * 8
            flat_ref[at : at + 8, 0:LANES] = jnp.where(sub < WIN, own, 0.0)
            flat_ref[at : at + 8, LANES:SQUEEZED] = jnp.where(sub < WIN, other, 0.0)
    spread = None
    for piece in pieces(flat_ref[...], 2):
        part = nt(piece, ones_ref[...])
        spread = part if spread is None else spread + part
    wide_ref[0] = spread
    for h in range(HEADS):
        total = jnp.zeros((8, SPREAD), F32)
        for jy in range(WIN):
            block = wide_ref[0, h * 56 + jy * 8 : h * 56 + jy * 8 + 8, :]
            total = total + pltpu.roll(block, 13 * (6 - jy), 1)
        line = jnp.zeros((1, SPREAD), F32)
        for jz in range(WIN):
            line = line + pltpu.roll(total, 6 - jz, 1)[jz : jz + 1]
        for c in range(SPREAD // 128):
            put(384 + h * 18 + c, line[:, c * 128 : c * 128 + 128])


def window_at(t):
    inner = jnp.where(t < 5, t, t - 7)
    edge = t - 5
    side_x = jnp.where(edge < 4, 3, edge - 4)
    side_y = jnp.where(edge < 4, edge, 3)
    is_edge = (t >= 5) & (t < 12)
    return jnp.where(is_edge, side_x, inner // 3), jnp.where(is_edge, side_y, inner % 3)


def whole_kernel(
    factor,
    x_hbm,
    dy_hbm,
    gain_ref,
    shift_ref,
    table_ref,
    ones_ref,
    w_raw_ref,
    b_raw_ref,
    k_feat_ref,
    q_feat_ref,
    w_proj_ref,
    out_hbm,
    result_ref,
    w_all_ref,
    w_kv_ref,
    b_col_ref,
    b_kv_ref,
    w_qkv_ref,
    wide_table_ref,
    bias_ref,
    acc_ref,
    e_ref,
    ds_ref,
    q_ref,
    do_ref,
    ln_ref,
    gq_ref,
    wide_ref,
    flat_ref,
    wq_ref,
    wkv_ref,
    proj_ref,
    rows_ref,
    ext_ref,
    win_ref,
    send_f_ref,
    dyb_ref,
    dx_ref,
    back_f_ref,
    out_ext_ref,
    fwd_send_ref,
    fwd_recv_ref,
    ret_send_ref,
    ret_recv_ref,
    pay_ref,
    near_ref,
    part_ref,
    far_ref,
    load_sem,
    halo_send,
    halo_recv,
    fwd_send,
    fwd_recv,
    ret_send,
    ret_recv,
    out_sem,
    edge_send,
    edge_recv,
    near_send,
    near_recv,
    far_send,
    far_recv,
    share_send,
    share_recv,
    all_send,
    all_recv,
):
    nx, ny, nz = lax.axis_size("gx"), lax.axis_size("gy"), lax.axis_size("gz")
    gx, gy, gz = lax.axis_index("gx"), lax.axis_index("gy"), lax.axis_index("gz")
    plane = nx * ny
    spot = gx * ny + gy
    cells_x, cells_y = x_hbm.shape[0], x_hbm.shape[1]
    total = (cells_x // WIN) * (cells_y // WIN)

    def peer_z(k):
        return {"gz": lax.rem(gz + k, nz)}

    def peer_xy(k):
        other = lax.rem(spot + k, plane)
        return {"gx": other // ny, "gy": lax.rem(other, ny)}

    barrier = pltpu.get_barrier_semaphore()
    for k in range(1, nz):
        pl.semaphore_signal(barrier, inc=1, device_id=peer_z(k), device_id_type=MESH)
    for k in range(1, plane):
        pl.semaphore_signal(barrier, inc=1, device_id=peer_xy(k), device_id_type=MESH)

    def load(a):
        source = (x_hbm, dy_hbm)[a]
        return pltpu.make_async_copy(
            source, ext_ref.at[a, pl.ds(0, cells_x), pl.ds(0, cells_y)], load_sem.at[a]
        )

    def halo(a, side):
        source = (x_hbm, dy_hbm)[a]
        px, py = ((1, 0), (0, 1), (1, 1))[side]
        from_x = pl.ds(0, SHIFT) if px else pl.ds(0, cells_x)
        from_y = pl.ds(0, SHIFT) if py else pl.ds(0, cells_y)
        to_x = pl.ds(cells_x, SHIFT) if px else pl.ds(0, cells_x)
        to_y = pl.ds(cells_y, SHIFT) if py else pl.ds(0, cells_y)
        return pltpu.make_async_remote_copy(
            src_ref=source.at[from_x, from_y],
            dst_ref=ext_ref.at[a, to_x, to_y],
            send_sem=halo_send.at[a, side],
            recv_sem=halo_recv.at[a, side],
            device_id={"gx": lax.rem(gx + nx - px, nx), "gy": lax.rem(gy + ny - py, ny)},
            device_id_type=MESH,
        )

    def fwd(t):
        return pltpu.make_async_remote_copy(
            src_ref=fwd_send_ref.at[t],
            dst_ref=fwd_recv_ref.at[t],
            send_sem=fwd_send,
            recv_sem=fwd_recv.at[t],
            device_id=peer_z(nz - 1),
            device_id_type=MESH,
        )

    def ret(t):
        return pltpu.make_async_remote_copy(
            src_ref=ret_send_ref.at[t],
            dst_ref=ret_recv_ref.at[t],
            send_sem=ret_send,
            recv_sem=ret_recv.at[t],
            device_id=peer_z(1),
            device_id_type=MESH,
        )

    def edge(side):
        px, py = ((1, 0), (0, 1), (1, 1))[side]
        from_x = pl.ds(cells_x, SHIFT) if px else pl.ds(SHIFT, cells_x - SHIFT)
        from_y = pl.ds(cells_y, SHIFT) if py else pl.ds(SHIFT, cells_y - SHIFT)
        to_x = pl.ds(0, SHIFT) if px else pl.ds(SHIFT, cells_x - SHIFT)
        to_y = pl.ds(0, SHIFT) if py else pl.ds(SHIFT, cells_y - SHIFT)
        return pltpu.make_async_remote_copy(
            src_ref=out_ext_ref.at[from_x, from_y],
            dst_ref=out_hbm.at[to_x, to_y],
            send_sem=edge_send.at[side],
            recv_sem=edge_recv.at[side],
            device_id={"gx": lax.rem(gx + px, nx), "gy": lax.rem(gy + py, ny)},
            device_id_type=MESH,
        )

    def store_out(n):
        first, last = ((SHIFT, 17), (24, cells_x), (17, 24))[n]
        rows = pl.ds(first, last - first)
        inner_y = pl.ds(SHIFT, cells_y - SHIFT)
        return pltpu.make_async_copy(out_ext_ref.at[rows, inner_y], out_hbm.at[rows, inner_y], out_sem.at[n])

    def wait_bytes(like, sem):
        pltpu.make_async_copy(like, like, sem).wait()

    def near(k):
        return pltpu.make_async_remote_copy(
            src_ref=pay_ref.at[lax.rem(gz + k, nz)],
            dst_ref=near_ref.at[gz],
            send_sem=near_send,
            recv_sem=near_recv,
            device_id=peer_z(k),
            device_id_type=MESH,
        )

    def far(k):
        return pltpu.make_async_remote_copy(
            src_ref=part_ref.at[lax.rem(spot + k, plane)],
            dst_ref=far_ref.at[spot],
            send_sem=far_send,
            recv_sem=far_recv,
            device_id=peer_xy(k),
            device_id_type=MESH,
        )

    def share(k):
        return pltpu.make_async_remote_copy(
            src_ref=result_ref.at[gz, spot],
            dst_ref=result_ref.at[gz, spot],
            send_sem=share_send,
            recv_sem=share_recv,
            device_id=peer_xy(k),
            device_id_type=MESH,
        )

    def final(k):
        return pltpu.make_async_remote_copy(
            src_ref=result_ref.at[gz],
            dst_ref=result_ref.at[gz],
            send_sem=all_send,
            recv_sem=all_recv,
            device_id=peer_z(k),
            device_id_type=MESH,
        )

    load(0).start()
    load(1).start()
    acc_ref[...] = jnp.zeros_like(acc_ref)
    e_ref[...] = jnp.zeros_like(e_ref)
    ds_ref[...] = jnp.zeros_like(ds_ref)
    q_ref[...] = jnp.zeros_like(q_ref)
    do_ref[...] = jnp.zeros_like(do_ref)
    wq_ref[...] = jnp.zeros_like(wq_ref)
    wkv_ref[...] = jnp.zeros_like(wkv_ref)
    proj_ref[...] = jnp.zeros_like(proj_ref)
    rows_ref[...] = jnp.zeros_like(rows_ref)
    gq_ref[...] = jnp.zeros_like(gq_ref)
    ln_ref[...] = jnp.zeros_like(ln_ref)
    dyb_ref[...] = jnp.zeros_like(dyb_ref)
    send_f_ref[...] = jnp.zeros_like(send_f_ref)
    pay_ref[...] = jnp.zeros_like(pay_ref)
    for t in range(total):
        dx_ref[t, 0:8, :] = jnp.zeros((8, FEATS), F32)
        dx_ref[t, 360:368, :] = jnp.zeros((8, FEATS), F32)
    gq_ref[0:96, 0:288] = w_raw_ref[...].astype(F32)
    wide_w = gq_ref[...]
    lane = lax.broadcasted_iota(jnp.int32, (96, 128), 1)
    w_all_ref[0:288, :] = wide_w.T[0:288, 0:96].astype(BF16)
    eye = lax.broadcasted_iota(jnp.int32, (96, 96), 0) == lax.broadcasted_iota(jnp.int32, (96, 96), 1)
    w_all_ref[288:384, :] = eye.astype(F32).astype(BF16)
    turns = [wide_w if n == 0 else pltpu.roll(wide_w, LANES - 96 * n, 1) for n in range(3)]
    for n in range(3):
        piece = jnp.where(lane < FEATS, turns[n][0:96, 0:128], 0.0).astype(BF16)
        w_qkv_ref[:, n * 128 : n * 128 + 128] = piece
        if n:
            w_kv_ref[:, n * 128 - 128 : n * 128] = piece
    gq_ref[...] = jnp.zeros_like(gq_ref)
    gq_ref[:, 0:288] = jnp.broadcast_to(b_raw_ref[...], (128, 288))
    wide_b = gq_ref[...]
    b_col_ref[...] = wide_b.T
    for n in (1, 2):
        piece = jnp.where(lane[0:1] < FEATS, pltpu.roll(wide_b, LANES - 96 * n, 1)[0:1, 0:128], 0.0)
        b_kv_ref[:, n * 128 - 128 : n * 128] = k_feat_ref[:, n * 128 - 128 : n * 128] + piece
    gq_ref[...] = jnp.zeros_like(gq_ref)
    wide_table_ref[...] = jnp.zeros_like(wide_table_ref)
    wide_table_ref[0:HEADS, 0:TABLE] = table_ref[...]
    pl.semaphore_wait(barrier, nz - 1 + plane - 1)
    for a in range(2):
        for side in range(3):
            halo(a, side).start()
    load(0).wait()
    load(1).wait()

    def gather(t):
        wx, wy = window_at(t)
        for a in range(2):
            for ix in range(WIN):
                for iy in range(WIN):
                    n = ix * WIN + iy
                    tile = ext_ref[a, wx * WIN + SHIFT + ix, wy * WIN + SHIFT + iy].astype(F32)
                    win_ref[t, a, pl.ds(4 * n, 4), :] = tile[3:7]
                    send_f_ref[pl.ds(3 * n, 3), :] = tile[0:3]
            fwd_send_ref[t, a] = send_f_ref[...].astype(BF16)
        fwd(t).start()

    def first_gather(t, carry):
        gather(t)
        return carry

    lax.fori_loop(0, AHEAD, first_gather, 0)
    expand_table(wide_table_ref, ones_ref, bias_ref, wide_ref, flat_ref)

    def compute(t):
        wx, wy = window_at(t)
        last_x = (gx == nx - 1) & (wx == cells_x // WIN - 1)
        last_y = (gy == ny - 1) & (wy == cells_y // WIN - 1)
        last_z = gz == nz - 1
        fwd(t).wait_recv()
        for a in range(2):
            win_ref[t, a, OWN:ROWS, :] = fwd_recv_ref[t, a].astype(F32)[0 : ROWS - OWN]
        x = win_ref[t, 0]
        mean = jnp.mean(x, -1, keepdims=True)
        centered = x - mean
        rstd = lax.rsqrt(jnp.mean(centered * centered, -1, keepdims=True) + 1e-05)
        xhat = centered * rstd
        ln_ref[0:ROWS, :] = (xhat * gain_ref[...] + shift_ref[...]).astype(BF16)

        across = nt(w_all_ref[...], ln_ref[...])
        q_t = ((across[0:96] + b_col_ref[0:96, 0:1]) * (SCALE * LOG2E)).astype(BF16)
        k_t = (across[96:192] + b_col_ref[96:192, 0:1]).astype(BF16)
        v_t = (across[192:288] + b_col_ref[192:288, 0:1]).astype(BF16)
        ln_t = across[288:384].astype(BF16)
        marks = (
            q_feat_ref[0] * last_x.astype(F32)
            + q_feat_ref[1] * last_y.astype(F32)
            + q_feat_ref[2] * last_z.astype(F32)
        ).astype(BF16)
        for h in range(HEADS):
            q_ref[h * HDIM : (h + 1) * HDIM, h * LANES : (h + 1) * LANES] = q_t[h * HDIM : (h + 1) * HDIM]
            q_ref[96:112, h * LANES : (h + 1) * LANES] = marks
        kv = nn(ln_ref[0:ROWS, :], w_kv_ref[...]) + b_kv_ref[...]
        k = kv[:, 0:128].astype(BF16)
        v = kv[:, 128:256].astype(BF16)
        dyb_ref[0:ROWS, :] = win_ref[t, 1].astype(BF16)
        dy = dyb_ref[...]
        do_t = nt(w_proj_ref[...], dy)

        for h in range(HEADS):
            do_ref[h * HDIM : (h + 1) * HDIM, h * LANES : (h + 1) * LANES] = do_t[h * HDIM : (h + 1) * HDIM].astype(BF16)
        for u in range(0, HEADS * LANES, 256):
            at = pl.ds(u, min(256, HEADS * LANES - u))
            s = nn(k, q_ref[:, at]) + bias_ref[:, at]
            dp = nn(v, do_ref[:, at])
            e = jnp.exp2(s - jnp.max(s, 0, keepdims=True))
            e = e * (1.0 / jnp.sum(e, 0, keepdims=True))
            e_ref[0:ROWS, at] = e.astype(BF16)
            ds = e * (dp - jnp.sum(e * dp, 0, keepdims=True))
            acc_ref[:, at] += ds
            ds_ref[0:ROWS, at] = ds.astype(BF16)
        att = []
        for h in range(HEADS):
            at = pl.ds(h * LANES, LANES)
            att.append(nn(v_t[h * HDIM : (h + 1) * HDIM], e_ref[:, at]).astype(BF16))
            gq_ref[h * HDIM : (h + 1) * HDIM, :] = nn(k_t[h * HDIM : (h + 1) * HDIM], ds_ref[:, at]) * SCALE
        att = jnp.concatenate(att, 0)
        proj_ref[...] += nn(att, dy)
        grad_v = nt(e_ref[0:ROWS, :], do_ref[...])
        grad_k = nt(ds_ref[0:ROWS, :], q_ref[0:96, :]) * (1.0 / LOG2E)
        gq = gq_ref[...]
        wq_ref[0:96, 0:96] += nn(gq[0:96].astype(BF16), ln_ref[...])
        turned = gq.T[0:ROWS, 0:96]
        grad_q = turned.astype(BF16)
        grad_v = grad_v[:, 0:96]
        k_b = grad_k.astype(BF16)
        v_b = grad_v.astype(BF16)
        wkv_ref[:, 0:96] += nn(ln_t[:, 0:ROWS], k_b)
        wkv_ref[:, 128:224] += nn(ln_t[:, 0:ROWS], v_b)
        grad_in = (
            nt(grad_q, w_qkv_ref[:, 0:96])
            + nt(k_b, w_qkv_ref[:, 128:224])
            + nt(v_b, w_qkv_ref[:, 256:352])
        )
        for n, term in enumerate((turned, grad_k, grad_v, xhat * grad_in, grad_in)):
            rows_ref[n] += jnp.sum(term.reshape(ROWS // 8, 8, 96), 0)
        dhat = grad_in * gain_ref[...]
        first = jnp.mean(dhat, -1, keepdims=True)
        second = jnp.mean(dhat * xhat, -1, keepdims=True)
        dx_ref[t, 8 : 8 + ROWS, :] = win_ref[t, 1] + rstd * (dhat - first - xhat * second)
        ret_send_ref[t] = dx_ref[t, 8 + OWN : 8 + OWN + 160, :].astype(BF16)
        ret(t).start()

    sub = lax.broadcasted_iota(jnp.int32, (8, FEATS), 0)

    def merge(t):
        wx, wy = window_at(t)
        ret(t).wait_recv()
        back_f_ref[...] = ret_recv_ref[t].astype(F32)
        for ix in range(WIN):
            for iy in range(WIN):
                n = ix * WIN + iy
                low = back_f_ref[pl.ds(3 * n, 8), :]
                high = dx_ref[t, pl.ds(5 + 4 * n, 8), :]
                tile = jnp.where(sub < SHIFT, low, high).astype(BF16)
                out_ext_ref[wx * WIN + SHIFT + ix, wy * WIN + SHIFT + iy] = tile[0:7]

    def step(t, carry):
        @pl.when(t == 5 - AHEAD)
        def _():
            for a in range(2):
                for side in range(3):
                    halo(a, side).wait_recv()

        @pl.when(t + AHEAD < total)
        def _():
            gather(t + AHEAD)

        compute(t)

        @pl.when(t >= LAG)
        def _():
            merge(t - LAG)

        return carry

    lax.fori_loop(0, total, step, 0)

    block = plane * QUAD

    def put(row, value):
        while value.shape[0]:
            at = row % QUAD
            count = min(QUAD - at, value.shape[0])
            pay_ref[row // block, row % block // QUAD, at : at + count, 0 : value.shape[1]] = value[0:count]
            value = value[count:]
            row += count

    table_block = 384 // block
    put(0, wq_ref[...].T[0:96, 0:96])
    put(96, wkv_ref[:, 0:96])
    put(192, wkv_ref[:, 128:224])
    put(288, proj_ref[...])
    for k in range(1, nz):
        @pl.when(lax.rem(gz + k, nz) != table_block)
        def _():
            near(k).start()

    for side in range(3):
        edge(side).start()
    store_out(0).start()
    store_out(1).start()
    for n in range(5):
        put(438 + n, jnp.sum(rows_ref[n], 0, keepdims=True))
    fold_table(acc_ref, ones_ref, wide_ref, flat_ref, put)
    for k in range(1, nz):
        @pl.when(lax.rem(gz + k, nz) == table_block)
        def _():
            near(k).start()
    near_ref[gz] = pay_ref[gz]

    def last_merge(t, carry):
        merge(t)
        return carry

    lax.fori_loop(total - LAG, total, last_merge, 0)
    store_out(2).start()
    most_z = pl.ds(0, nz - 1)
    most_xy = pl.ds(0, plane - 1)
    wait_bytes(near_ref.at[most_z], near_recv)
    part_ref[...] = jnp.sum(near_ref[...], 0)
    for k in range(1, plane):
        far(k).start()
    far_ref[spot] = part_ref[spot]
    wait_bytes(far_ref.at[most_xy], far_recv)
    result_ref[gz, spot] = jnp.sum(far_ref[...], 0) * factor
    for k in range(1, plane):
        share(k).start()
    wait_bytes(far_ref.at[most_xy], share_recv)
    for k in range(1, nz):
        final(k).start()
    for n in range(3):
        store_out(n).wait()
    for side in range(3):
        edge(side).wait()
    for a in range(2):
        for side in range(3):
            halo(a, side).wait_send()
    wait_bytes(fwd_send_ref, fwd_send)
    wait_bytes(ret_send_ref, ret_send)
    wait_bytes(near_ref.at[most_z], near_send)
    wait_bytes(far_ref.at[most_xy], far_send)
    wait_bytes(far_ref.at[most_xy], share_send)
    wait_bytes(near_ref.at[most_z], all_send)
    wait_bytes(near_ref.at[most_z], all_recv)


def whole_call(factor, inputs, d_out, gain, shift, table, w_qkv, b_qkv, w_proj):
    cells_x, cells_y, cells_z, _ = inputs.shape
    count = (cells_x // WIN) * (cells_y // WIN)
    nz, plane = lax.axis_size("gz"), lax.axis_size("gx") * lax.axis_size("gy")
    ones = jnp.asarray(squeeze_ones(), BF16)
    consts = (gain[None, :], shift[None, :], table, ones, w_qkv, b_qkv[None, :])
    consts += (jnp.asarray(key_features()), jnp.asarray(query_features()), w_proj)
    outs = (
        jax.ShapeDtypeStruct(inputs.shape, BF16),
        jax.ShapeDtypeStruct((nz, plane, QUAD, 128), F32),
    )
    anywhere = pl.BlockSpec(memory_space=pl.ANY)
    inside = pl.BlockSpec(memory_space=pltpu.VMEM)
    dma = pltpu.SemaphoreType.DMA
    return pl.pallas_call(
        functools.partial(whole_kernel, factor),
        in_specs=[anywhere] * 2 + [inside] * len(consts),
        out_specs=[anywhere, inside],
        out_shape=outs,
        scratch_shapes=[
            pltpu.VMEM((LANES, FEATS), BF16),
            pltpu.VMEM((96, 256), BF16),
            pltpu.VMEM((LANES, 128), F32),
            pltpu.VMEM((ROWS, 256), F32),
            pltpu.VMEM((96, LANES), BF16),
            pltpu.VMEM((8, SPREAD), F32),
            pltpu.VMEM((ROWS, HEADS * LANES), F32),
            pltpu.VMEM((ROWS, HEADS * LANES), F32),
            pltpu.VMEM((LANES, HEADS * LANES), BF16),
            pltpu.VMEM((LANES, HEADS * LANES), BF16),
            pltpu.VMEM((128, HEADS * LANES), BF16),
            pltpu.VMEM((128, HEADS * LANES), BF16),
            pltpu.VMEM((LANES, FEATS), BF16),
            pltpu.VMEM((128, LANES), F32),
            pltpu.VMEM((3, HEADS * 56, SPREAD), F32),
            pltpu.VMEM((HEADS * 56, SQUEEZED), F32),
            pltpu.VMEM((128, 128), F32),
            pltpu.VMEM((96, 256), F32),
            pltpu.VMEM((96, 96), F32),
            pltpu.VMEM((5, 8, 96), F32),
            pltpu.VMEM((2, cells_x + SHIFT, cells_y + SHIFT, cells_z, FEATS), BF16),
            pltpu.VMEM((count, 2, ROWS, FEATS), F32),
            pltpu.VMEM((160, FEATS), F32),
            pltpu.VMEM((LANES, FEATS), BF16),
            pltpu.VMEM((count, 368, FEATS), F32),
            pltpu.VMEM((160, FEATS), F32),
            pltpu.VMEM((cells_x + SHIFT, cells_y + SHIFT, cells_z, FEATS), BF16),
            pltpu.VMEM((count, 2, 160, FEATS), BF16),
            pltpu.VMEM((count, 2, 160, FEATS), BF16),
            pltpu.VMEM((count, 160, FEATS), BF16),
            pltpu.VMEM((count, 160, FEATS), BF16),
            pltpu.VMEM((nz, plane, QUAD, 128), F32),
            pltpu.VMEM((nz, plane, QUAD, 128), F32),
            pltpu.VMEM((plane, QUAD, 128), F32),
            pltpu.VMEM((plane, QUAD, 128), F32),
            dma((2,)),
            dma((2, 3)),
            dma((2, 3)),
            dma,
            dma((count,)),
            dma,
            dma((count,)),
            dma((3,)),
            dma((3,)),
            dma((3,)),
            dma,
            dma,
            dma,
            dma,
            dma,
            dma,
            dma,
            dma,
        ],
        compiler_params=pltpu.CompilerParams(
            vmem_limit_bytes=56 << 20, collective_id=0, has_side_effects=True
        ),
    )(inputs, d_out, *consts)


def shards(inputs, d_out, gain, shift, w_qkv, b_qkv, w_proj, rel_bias):
    count = inputs.size // FEATS * lax.axis_size("gx") * lax.axis_size("gy") * lax.axis_size("gz")
    factor = float(count) ** -0.5
    field, sums = whole_call(factor, inputs, d_out, gain, shift, rel_bias, w_qkv, b_qkv, w_proj)
    sums = sums.reshape(-1, 128)
    weight = jnp.concatenate([sums[0:96, :96], sums[96:192, :96], sums[192:288, :96]], 1)
    proj = sums[288:384, :96]
    rel = sums[384:438].reshape(HEADS, SPREAD)[:, :TABLE]
    bias = sums[438:441, :96].reshape(-1)
    return field, weight, bias, proj, rel, sums[441, :96], sums[442, :96]


def solution(mesh):
    placed = (P("gx", "gy", "gz", None), P("gx", "gy", "gz", None), P(), P(), P(), P(), P(), P())
    return jax.shard_map(
        shards,
        mesh=mesh,
        in_specs=placed,
        out_specs=(P("gx", "gy", "gz", None), P(), P(), P(), P(), P(), P()),
        check_vma=False,
    )
```
